512 devices in a mesh: dom: 64 (over x, z), split: 8 (over y, core).
Axes of the slice: x: 4, y: 4, z: 16, core: 2. Of those that a mesh axis runs over, the one named last changes fastest.
Arguments:
- modes_now: float32 [64, 4096, 128], P('split', 'dom'), may hold values from -6 to 6
- modes_prev: float32 [64, 4096, 128], P('split', 'dom'), may hold values from -6 to 6
- z_extent: int32 [64], P('dom'), may hold values from 16 to 64, as said below
- lower_nbr: int32 [64], P('dom'), may hold values from -1 to 63, as said below
- upper_nbr: int32 [64], P('dom'), may hold values from -1 to 63
- x_shift: int32 [64, 2], P('dom'), may hold values from -32 to 32, as said below
- y_shift: int32 [64, 2], P('dom'), may hold values from -32 to 32, as said below
Outputs:
- modes_next: float32 [64, 4096, 128], P('split', 'dom')
- modes_cur: float32 [64, 4096, 128], P('split', 'dom')
- pressure: float32 [64, 4096, 128], P('split', 'dom')
The draws below stay inside these ranges and needn't reach their ends.
Inputs may be any that keep to these rules, and one draw needn't show every extreme that they name: `z_extent`: at least one cuboid reaches the full 64 slots. Cuboids form chains: if upper_nbr[a] = b then lower_nbr[b] = a, and no cuboid is its own neighbour. If upper_nbr[a] = b then x_shift[a, 1] = -x_shift[b, 0]; zero at walls. If upper_nbr[a] = b then y_shift[a, 1] = -y_shift[b, 0]; zero at walls.
All inputs are finite; a program needn't handle non-finite values.
Results may differ from the reference program's by a relative error of at most 0.0003.
Values sent between devices are 32-bit elements; how exact they have to be, the bound alone decides.
A program may use at most 64 MiB of HBM per device.

```python
import jax
import jax.numpy as jnp
from jax import lax

NX = 64
NY = 128
ZC = 64
STEPS = 2
GROUPS = 64
TOTALZ = 4096


def chains(key):
    base = jax.random.fold_in(key, 7)
    order = jax.random.permutation(base, GROUPS).astype(jnp.int32)
    position = jnp.arange(GROUPS)
    cut = (jax.random.randint(jax.random.fold_in(base, 1), (GROUPS,), 0, 4) == 0) & (position > 0)
    link = jnp.logical_not(cut) & (position < GROUPS - 1)
    following = jnp.roll(order, -1)
    preceding = jnp.roll(order, 1)
    link_before = jnp.roll(link, 1) & (position > 0)
    upper = jnp.zeros((GROUPS,), jnp.int32).at[order].set(jnp.where(link, following, -1).astype(jnp.int32))
    lower = jnp.zeros((GROUPS,), jnp.int32).at[order].set(jnp.where(link_before, preceding, -1).astype(jnp.int32))
    move_x = jax.random.randint(jax.random.fold_in(base, 2), (GROUPS,), -(NX // 2), NX // 2 + 1)
    move_y = jax.random.randint(jax.random.fold_in(base, 3), (GROUPS,), -(NY // 4), NY // 4 + 1)
    move_x = jnp.where(position == 0, NX // 2, move_x).astype(jnp.int32)
    move_y = jnp.where(position == 0, NY // 4, move_y).astype(jnp.int32)
    up_x = jnp.where(link, move_x, 0).astype(jnp.int32)
    low_x = jnp.where(link_before, -jnp.roll(move_x, 1), 0).astype(jnp.int32)
    up_y = jnp.where(link, move_y, 0).astype(jnp.int32)
    low_y = jnp.where(link_before, -jnp.roll(move_y, 1), 0).astype(jnp.int32)
    shift_x = jnp.zeros((GROUPS, 2), jnp.int32).at[order].set(jnp.stack([low_x, up_x], axis=1))
    shift_y = jnp.zeros((GROUPS, 2), jnp.int32).at[order].set(jnp.stack([low_y, up_y], axis=1))
    return (lower, upper, shift_x, shift_y)


def draw_lower_nbr(key, part):
    return chains(key)[0]


def draw_upper_nbr(key, part):
    return chains(key)[1]


def draw_x_shift(key, part):
    return chains(key)[2]


def draw_y_shift(key, part):
    return chains(key)[3]


def draw_z_extent(key, part):
    base = jax.random.fold_in(key, 3)
    extent = jax.random.randint(base, (GROUPS,), ZC // 4, ZC + 1).astype(jnp.int32)
    spot = jax.random.randint(jax.random.fold_in(base, 1), (), 0, GROUPS)
    return extent.at[spot].set(ZC).astype(jnp.int32)


def shard_levels(own_key, shape, split, low, largest):
    def one(dim, parts):
        heights = jax.random.uniform(jax.random.fold_in(jax.random.fold_in(own_key, 6), dim), (parts,), jnp.float32, low / len(split), largest / len(split))
        return jnp.repeat(jnp.exp(heights), shape[dim] // parts).reshape((-1,) + (1,) * (len(shape) - dim - 1))

    level = one(*split[0])
    for cut in split[1:]:
        level = level * one(*cut)
    return level


def gaussian(own_key, shape, spread, most, split=(), kind=jnp.bfloat16):
    values = spread * jax.random.normal(own_key, shape, jnp.float32)
    if split:
        values = values * shard_levels(own_key, shape, split, -0.22, 0.18)
    return jnp.clip(values, -most, most).astype(kind)


def setup_inputs(seed: int = 0) -> dict:
    seeds = jax.random.split(jax.random.key(seed), 8)
    return {
        "modes_now": gaussian(seeds[0], (NX, TOTALZ, NY), 1.0, 6.0, ((0, 8), (1, 64)), jnp.float32),
        "modes_prev": gaussian(seeds[1], (NX, TOTALZ, NY), 1.0, 6.0, ((0, 8), (1, 64)), jnp.float32),
        "z_extent": draw_z_extent(jax.random.fold_in(seeds[7], 71), 0),
        "lower_nbr": draw_lower_nbr(jax.random.fold_in(seeds[7], 71), 0),
        "upper_nbr": draw_upper_nbr(jax.random.fold_in(seeds[7], 71), 0),
        "x_shift": draw_x_shift(jax.random.fold_in(seeds[7], 71), 0),
        "y_shift": draw_y_shift(jax.random.fold_in(seeds[7], 71), 0),
    }


HIGH = lax.Precision.HIGHEST
STENCIL = (-490.0 / 180.0, 270.0 / 180.0, -27.0 / 180.0, 2.0 / 180.0)
COURANT = 0.5

def cosine_table(kk, xx, length):
    scale = jnp.where(kk == 0, jnp.sqrt(1.0 / length), jnp.sqrt(2.0 / length))
    return scale * jnp.cos(jnp.pi * kk * (xx + 0.5) / length)

def square_table(count):
    index = jnp.arange(count).astype(jnp.float32)
    return cosine_table(index[:, None], index[None, :], jnp.float32(count))

def shifted(face, rows, move_y):
    count = face.shape[0]
    width = face.shape[2]
    cols = jnp.arange(width).astype(jnp.int32) + move_y
    rows_ok = (rows >= 0) & (rows < count)
    cols_ok = (cols >= 0) & (cols < width)
    picked = jnp.take(face, jnp.clip(rows, 0, count - 1).astype(jnp.int32), axis=0)
    picked = jnp.take(picked, jnp.clip(cols, 0, width - 1).astype(jnp.int32), axis=2)
    mask = (rows_ok[:, None, None] & cols_ok[None, None, :]).astype(jnp.float32)
    return (picked, mask)

def aligned(face, move_x, move_y):
    rows = jnp.arange(NX).astype(jnp.int32) + move_x
    return shifted(face, rows, move_y)

def z_tables(extent):
    zidx = jnp.arange(ZC).astype(jnp.int32)
    live = zidx < extent
    kz = zidx.astype(jnp.float32)
    lenf = extent.astype(jnp.float32)
    ztable = jnp.where(live[:, None] & live[None, :], cosine_table(kz[:, None], kz[None, :], lenf), 0.0)
    rows = jnp.array([0, 1, 2, -3, -2, -1], jnp.int32) + jnp.where(jnp.arange(6) >= 3, extent, 0).astype(jnp.int32)
    onerow = (zidx[None, :] == rows[:, None]).astype(jnp.float32)
    row_table = jnp.dot(ztable, onerow.T, precision=HIGH, preferred_element_type=jnp.float32)
    kx = jnp.arange(NX).astype(jnp.float32)
    ky = jnp.arange(NY).astype(jnp.float32)
    freq = COURANT * jnp.pi * jnp.sqrt((kx / NX)[:, None, None] ** 2 + (kz / lenf)[None, :, None] ** 2 + (ky / NY)[None, None, :] ** 2)
    twice_cos = 2.0 * jnp.cos(freq)
    gain = jnp.sinc(freq / (2.0 * jnp.pi)) ** 2
    return (ztable, row_table, twice_cos, gain)

def interface(lower_face, upper_face, from_lower, from_upper, has_lower, has_upper):
    low_rows = []
    for jj in range(3):
        total = jnp.zeros_like(lower_face[..., 0, :])
        for mm in range(-3, 0):
            if abs(jj - mm) <= 3:
                total = total + STENCIL[abs(jj - mm)] * (from_lower[..., mm + 3, :] - lower_face[..., -1 - mm, :])
        low_rows.append(total)
    up_rows = []
    for aa in range(3):
        tt = aa - 3
        total = jnp.zeros_like(upper_face[..., 0, :])
        for mm in range(3):
            if abs(tt - mm) <= 3:
                total = total + STENCIL[abs(tt - mm)] * (from_upper[..., mm, :] - upper_face[..., 2 - mm, :])
        up_rows.append(total)
    low = jnp.stack(low_rows, axis=-2) * has_lower
    upp = jnp.stack(up_rows, axis=-2) * has_upper
    return COURANT ** 2 * jnp.concatenate([low, upp], axis=-2)

def reference(modes_now, modes_prev, z_extent, lower_nbr, upper_nbr, x_shift, y_shift):
    xtable = square_table(NX)
    ytable = square_table(NY)
    zidx = jnp.arange(ZC).astype(jnp.int32)

    def to_groups(arr):
        return arr.reshape(NX, GROUPS, ZC, NY).transpose(1, 0, 2, 3)

    def masked(arr, extent):
        return arr * (zidx < extent).astype(jnp.float32)[None, :, None]
    now = lax.map(lambda a: masked(a[0], a[1]), (to_groups(modes_now), z_extent))
    prev = lax.map(lambda a: masked(a[0], a[1]), (to_groups(modes_prev), z_extent))

    def strip_of(args):
        mode, extent = args
        ztable, row_table, twice_cos, gain = z_tables(extent)
        part = jnp.einsum('kr,xky->xry', row_table, mode, precision=HIGH, preferred_element_type=jnp.float32)
        part = jnp.einsum('xrk,ky->xry', part, ytable, precision=HIGH, preferred_element_type=jnp.float32)
        return jnp.einsum('kx,kry->xry', xtable, part, precision=HIGH, preferred_element_type=jnp.float32)
    has_lower = (lower_nbr >= 0).astype(jnp.float32)[:, None, None, None]
    has_upper = (upper_nbr >= 0).astype(jnp.float32)[:, None, None, None]
    low_index = jnp.maximum(lower_nbr, 0).astype(jnp.int32)
    up_index = jnp.maximum(upper_nbr, 0).astype(jnp.int32)
    for step in range(STEPS):
        strips = lax.map(strip_of, (now, z_extent))
        lower_face = strips[:, :, 0:3]
        upper_face = strips[:, :, 3:6]
        from_lower, mask_low = jax.vmap(aligned)(upper_face[low_index], x_shift[:, 0], y_shift[:, 0])
        from_upper, mask_up = jax.vmap(aligned)(lower_face[up_index], x_shift[:, 1], y_shift[:, 1])
        forcing = interface(lower_face, upper_face, from_lower, from_upper, has_lower * mask_low, has_upper * mask_up)

        def update(args):
            mode, older, force, extent = args
            ztable, row_table, twice_cos, gain = z_tables(extent)
            part = jnp.einsum('xry,ky->xrk', force, ytable, precision=HIGH, preferred_element_type=jnp.float32)
            part = jnp.einsum('kx,xry->kry', xtable, part, precision=HIGH, preferred_element_type=jnp.float32)
            fmodes = jnp.einsum('kr,xry->xky', row_table, part, precision=HIGH, preferred_element_type=jnp.float32)
            return twice_cos * mode - older + gain * fmodes
        newer = lax.map(update, (now, prev, forcing, z_extent))
        prev, now = (now, newer)

    def field_of(args):
        mode, extent = args
        ztable, row_table, twice_cos, gain = z_tables(extent)
        part = jnp.einsum('kz,xky->xzy', ztable, mode, precision=HIGH, preferred_element_type=jnp.float32)
        part = jnp.einsum('xzk,ky->xzy', part, ytable, precision=HIGH, preferred_element_type=jnp.float32)
        return jnp.einsum('kx,kzy->xzy', xtable, part, precision=HIGH, preferred_element_type=jnp.float32)
    field = lax.map(field_of, (now, z_extent))

    def back(arr):
        return arr.transpose(1, 0, 2, 3).reshape(NX, GROUPS * ZC, NY)
    return (back(now), back(prev), back(field))
```

```python
import functools
import math

import jax
import jax.numpy as jnp
import numpy as np
from jax import lax
from jax.experimental import pallas as pl
from jax.experimental.pallas import tpu as pltpu
from jax.sharding import PartitionSpec as P

F32 = jnp.float32
HIGH = lax.Precision.HIGHEST
XN, ZN, SN = 4, 16, 8
NX, NY, ZC = 64, 128, 64
QUARTER = 0.25
ST1, ST2, ST3 = 270.0 / 180.0, -27.0 / 180.0, 2.0 / 180.0
GAIN = [2.0 * (-1.0) ** n / math.factorial(2 * n + 2) for n in range(12)]
HALF_PI_2 = (math.pi / 2) ** 2


def dot(a, b):
    return jnp.dot(a, b, precision=HIGH, preferred_element_type=F32)


def dot_nt(a, b):
    return lax.dot_general(a, b, (((1,), (1,)), ((), ())), precision=HIGH, preferred_element_type=F32)


def gain_of(u):
    g = jnp.full(u.shape, GAIN[-1], F32)
    for c in GAIN[-2::-1]:
        g = g * u + c
    return g


def cos_table(k, x, length):
    n = k * (2.0 * x + 1.0)
    period = 4.0 * length
    rest = n - period * jnp.floor(n / period + 0.5)
    w = (math.pi / 2) * (rest / length)
    u = w * w
    scale = jnp.where(k == 0, jnp.sqrt(1.0 / length), jnp.sqrt(2.0 / length))
    return scale * (1.0 - 0.5 * u * gain_of(u))


def iota(shape, dim):
    return lax.broadcasted_iota(jnp.int32, shape, dim).astype(F32)


def low_rows(q1, q2, q3):
    return [ST1 * q1 + ST2 * q2 + ST3 * q3, ST2 * q1 + ST3 * q2, ST3 * q1]


def kernel(
    ext, low, upp, xs, ys, m0, m1, cx, cxt, cy,
    nxt, cur, prs,
    rt, rtt, ztt, mz, b1, gn, tc, h0, sscr, st, nb, near, sel, far, ab, xab, yab, g, hs, hb, e1, ge, yo, yr,
    nb_s, nb_r, near_s, near_r, far_s, far_r, ab_s, ab_r, h_s, h_r, y_s, y_r,
):
    dom, me = lax.axis_index("dom"), lax.axis_index("split")
    px, pz = dom // ZN, lax.rem(dom, ZN)

    def at(dx, dz):
        return lax.rem(px + dx + XN, XN) * ZN + lax.rem(pz + dz + ZN, ZN)

    def other(t):
        return lax.rem(me + t, SN)

    near_all = [(i, d) for i in range(XN) for d in range(-2, 3)]
    near_out = [p for p in near_all if p != (0, 0)]

    barrier = pltpu.get_barrier_semaphore()

    def greet(d, s):
        pl.semaphore_signal(barrier, inc=1, device_id=(d, s), device_id_type=pl.DeviceIdType.MESH)

    for i, d in near_out:
        greet(at(i, d), me)
    for k in range(1, 4):
        greet(at(0, 4 * k), me)
    for t in range(1, SN):
        greet(dom, other(t))

    started = []

    def send(src, dst, ss, rs, d, s):
        c = pltpu.make_async_remote_copy(
            src_ref=src, dst_ref=dst, send_sem=ss, recv_sem=rs, device_id=(d, s), device_id_type=pl.DeviceIdType.MESH
        )
        c.start()
        started.append(c)

    def arrived(dst, ss, rs):
        pltpu.make_async_remote_copy(
            src_ref=dst, dst_ref=dst, send_sem=ss, recv_sem=rs, device_id=(dom, me), device_id_type=pl.DeviceIdType.MESH
        ).wait_recv()

    length = ext[0].astype(F32)
    lowf, uppf = low[0].astype(F32), upp[0].astype(F32)

    def row_of(r):
        return jnp.where(r < 3, r, r + (length - 6.0))

    k8, r8 = iota((8, ZC), 1), iota((8, ZC), 0)
    rtt[...] = jnp.where((k8 < length) & (r8 < 6), cos_table(k8, row_of(r8), jnp.full((8, ZC), length)), 0.0)
    k8, r8 = iota((ZC, 8), 0), iota((ZC, 8), 1)
    rt[...] = jnp.where((k8 < length) & (r8 < 6), cos_table(k8, row_of(r8), jnp.full((ZC, 8), length)), 0.0)

    def rows(i):
        return pl.ds(pl.multiple_of(i * ZC, ZC), ZC)

    kz = iota((ZC, NY), 0)
    live = kz < length

    def first(i, _):
        m = jnp.where(live, m0[rows(i), :], 0.0)
        mz[rows(i), :] = m
        sscr[pl.ds(pl.multiple_of(i * 8, 8), 8), :] = dot(rtt[...], m)
        return 0

    lax.fori_loop(0, 8, first, 0)

    def put_strip(step):
        for r in range(6):
            st[step, r] = sscr[pl.ds(r, 8, stride=8), :]

    put_strip(0)
    nb[0, 0] = jnp.full((8, 128), lowf)
    nb[0, 1] = jnp.full((8, 128), uppf)
    pl.semaphore_wait(barrier, len(near_out) + 3 + SN - 1)

    def half(d):
        return slice(3, 6) if d == 2 else slice(0, 3) if d == -2 else slice(0, 6)

    def send_near(step):
        for n, (i, d) in enumerate(near_all):
            if (i, d) == (0, 0):
                continue
            h = half(d)
            send(st.at[step, h], near.at[step, n, h], near_s.at[step, n], near_r.at[step, n], at(i, d), me)

    for k in range(1, 4):
        send(nb.at[0], nb.at[k], nb_s.at[k], nb_r.at[k], at(0, -4 * k), me)
    send_near(0)

    def matrices(c, n, move):
        row, col = iota((n, n), 0), iota((n, n), 1)
        put = (col == row + move).astype(F32)
        table = c[...]
        seen = ((col + move >= 0) & (col + move < n)).astype(F32)
        return dot_nt(dot(table, put), table), dot_nt(table * seen, table)

    for f in range(2):
        has = jnp.where(jnp.full((NX, NX), uppf if f else lowf) >= 0, QUARTER, 0.0)
        a, b = matrices(cx, NX, xs[0, f].astype(F32))
        xab[f, :, 0:NX] = a * has
        xab[f, :, NX : 2 * NX] = -b * has
        a, b = matrices(cy, NY, ys[0, f].astype(F32))
        yab[f, 0] = a
        yab[f, 1] = b

    lv = jnp.full((ZC, NY), length)
    flat = kz / lv
    flat = flat * flat + (iota((ZC, NY), 1) / NY) ** 2

    def second(i, _):
        kx = (me * 8 + i).astype(F32) / NX
        u = HALF_PI_2 * (flat + kx * kx)
        gain = gain_of(u)
        tw = 2.0 - u * gain
        m = mz[rows(i), :]
        base = tw * m - jnp.where(live, m1[rows(i), :], 0.0)
        gn[rows(i), :] = gain
        tc[rows(i), :] = tw
        b1[rows(i), :] = base
        h0[rows(i), :] = tw * base - m
        return 0

    lax.fori_loop(0, 8, second, 0)

    def turn(k, _):
        hs[k] = h0[pl.ds(k, 8, stride=ZC), :]
        return 0

    lax.fori_loop(0, ZC, turn, 0)

    def send_ab(step, w):
        for t in range(1, SN):
            send(ab.at[step, w, me], ab.at[step, w, me], ab_s.at[step, w, t], ab_r.at[step, w, t], dom, other(t))

    def put_ab(step, w, lo, up):
        ab[step, w, me, 0:3] = dot_nt(jnp.concatenate(lo, axis=0), yab[0, w]).reshape(3, 8, NY)
        ab[step, w, me, 3:6] = dot_nt(jnp.concatenate(up, axis=0), yab[1, w]).reshape(3, 8, NY)
        send_ab(step, w)

    def own_part(step):
        p = [st[step, r] for r in range(6)]
        put_ab(step, 1, low_rows(p[0], p[1], p[2]), low_rows(p[5], p[4], p[3])[::-1])

    def exchange(step):
        lo = [[jnp.zeros((8, NY), F32)] * 3 for _ in range(4)]
        up = [[jnp.zeros((8, NY), F32)] * 3 for _ in range(4)]
        for n, (i, d) in enumerate(near_all):
            if (i, d) == (0, 0):
                block = st.at[step]
            else:
                h = half(d)
                arrived(near.at[step, n, h], near_s.at[step, n], near_r.at[step, n])
                block = near.at[step, n]
            who = at(-i, -d).astype(F32)
            if d >= -1:
                b = [block[r] for r in range(3, 6)]
                for k in range(4):
                    hit = nb[k, 0] == who
                    lo[k] = [jnp.where(hit, v, a) for v, a in zip(b, lo[k])]
            if d <= 1:
                b = [block[r] for r in range(3)]
                for k in range(4):
                    hit = nb[k, 1] == who
                    up[k] = [jnp.where(hit, v, a) for v, a in zip(b, up[k])]
        for k in range(1, 4):
            for r in range(3):
                sel[step, k, r] = lo[k][r]
                sel[step, k, r + 3] = up[k][r]
            send(sel.at[step, k], far.at[step, k], far_s.at[step, k], far_r.at[step, k], at(0, 4 * k), me)
        q = lo[0] + up[0]
        for k in range(1, 4):
            arrived(far.at[step, k], far_s.at[step, k], far_r.at[step, k])
            q = [a + far[step, k, r] for r, a in enumerate(q)]
        put_ab(step, 0, low_rows(q[2], q[1], q[0]), low_rows(q[3], q[4], q[5])[::-1])
        for t in range(1, SN):
            src = other(SN - t)
            for w in range(2):
                arrived(ab.at[step, w, src], ab_s.at[step, w, t], ab_r.at[step, w, t])
        for r in range(6):
            rhs = jnp.concatenate([ab[step, w, :, r].reshape(NX, NY) for w in range(2)], axis=0)
            g[step, r * NX : (r + 1) * NX, :] = dot(xab[r // 3], rhs)
        g[step, 6 * NX :, :] = jnp.zeros((2 * NX, NY), F32)

    def forced(step, i):
        return gn[rows(i), :] * dot(rt[...], g[step, pl.ds(me * 8 + i, 8, stride=NX), :])

    own_part(0)
    for t in range(1, SN):
        dst = pl.multiple_of(other(t) * 8, 8)
        send(hs.at[pl.ds(dst, 8)], hb.at[me], h_s.at[t], h_r.at[t], dom, other(t))
    hb[me] = hs[pl.ds(pl.multiple_of(me * 8, 8), 8)]
    kk, zz = iota((ZC, ZC), 1), iota((ZC, ZC), 0)
    ztt[...] = jnp.where((kk < length) & (zz < length), cos_table(kk, zz, jnp.full((ZC, ZC), length)), 0.0)
    for k in range(1, 4):
        arrived(nb.at[k], nb_s.at[k], nb_r.at[k])
    exchange(0)

    def step_one(i, _):
        m = b1[rows(i), :] + forced(0, i)
        cur[rows(i), :] = m
        sscr[pl.ds(pl.multiple_of(i * 8, 8), 8), :] = dot(rtt[...], m)
        return 0

    lax.fori_loop(0, 8, step_one, 0)
    put_strip(1)
    send_near(1)
    own_part(1)

    for t in range(1, SN):
        arrived(hb.at[other(SN - t)], h_s.at[t], h_r.at[t])
    kx2 = (iota((NX, NY), 0) / NX) ** 2 + (iota((NX, NY), 1) / NY) ** 2

    def rowsum(step, j):
        c = rt[pl.ds(me * 8 + j, 1), :]
        total = c[:, 0:1] * g[step, 0:NX, :]
        for r in range(1, 6):
            total = total + c[:, r : r + 1] * g[step, r * NX : (r + 1) * NX, :]
        return total

    def early(j, _):
        z = jnp.full((NX, NY), (me * 8 + j).astype(F32)) / lv
        u = HALF_PI_2 * (kx2 + z * z)
        gain = gain_of(u)
        ge[j] = gain
        e1[j] = hb[:, j].reshape(NX, NY) + gain * (2.0 - u * gain) * rowsum(0, j)
        return 0

    lax.fori_loop(0, 8, early, 0)
    exchange(1)

    def late(j, _):
        out = dot(cxt[...], e1[j] + ge[j] * rowsum(1, j))
        yo[:, j] = out.reshape(SN, 8, NY)
        return 0

    lax.fori_loop(0, 8, late, 0)
    mine = pl.ds(pl.multiple_of(me * 64, 64), 64)
    for t in range(1, SN):
        send(yo.at[other(t)], yr.at[me], y_s.at[t], y_r.at[t], dom, other(t))
    yr[me] = yo[me]

    def step_two(i, _):
        nxt[rows(i), :] = tc[rows(i), :] * cur[rows(i), :] - mz[rows(i), :] + forced(1, i)
        return 0

    lax.fori_loop(0, 8, step_two, 0)
    for t in range(1, SN):
        arrived(yr.at[other(SN - t)], y_s.at[t], y_r.at[t])

    for i in range(8):
        y = yr[:, :, i].reshape(ZC, NY)
        prs[i * ZC : (i + 1) * ZC, :] = dot(dot(ztt[...], y), cy[...])

    for c in started:
        c.wait_send()


def table(n):
    k, x = np.arange(n)[:, None], np.arange(n)[None, :]
    return (np.where(k == 0, math.sqrt(1 / n), math.sqrt(2 / n)) * np.cos(math.pi * k * (x + 0.5) / n)).astype(np.float32)


def on_device(modes_now, modes_prev, z_extent, lower_nbr, upper_nbr, x_shift, y_shift):
    slab = modes_now.shape[0]
    flat = jax.ShapeDtypeStruct((slab * ZC, NY), F32)
    cx = table(NX)
    smem, vmem = pl.BlockSpec(memory_space=pltpu.SMEM), pl.BlockSpec(memory_space=pltpu.VMEM)
    v = lambda *s: pltpu.VMEM(s, F32)
    dma = pltpu.SemaphoreType.DMA
    outs = pl.pallas_call(
        kernel,
        out_shape=(flat,) * 3,
        in_specs=[smem] * 5 + [vmem] * 5,
        out_specs=(vmem,) * 3,
        scratch_shapes=[
            v(ZC, 8), v(8, ZC), v(ZC, ZC),
            v(512, NY), v(512, NY), v(512, NY), v(512, NY), v(512, NY), v(64, NY),
            v(2, 6, 8, NY), v(4, 2, 8, NY), v(2, 20, 6, 8, NY), v(2, 4, 6, 8, NY), v(2, 4, 6, 8, NY),
            v(2, 2, 8, 6, 8, NY), v(2, NX, 2 * NX), v(2, 2, NY, NY), v(2, 8 * NX, NY),
            v(ZC, 8, NY), v(8, 8, 8, NY), v(8, NX, NY), v(8, NX, NY), v(8, 8, 8, NY), v(8, 8, 8, NY),
            dma((4,)), dma((4,)), dma((2, 20)), dma((2, 20)), dma((2, 4)), dma((2, 4)),
            dma((2, 2, 8)), dma((2, 2, 8)), dma((8,)), dma((8,)), dma((8,)), dma((8,)),
        ],
        compiler_params=pltpu.CompilerParams(collective_id=0, has_side_effects=True),
    )(
        z_extent, lower_nbr, upper_nbr, x_shift, y_shift,
        modes_now.reshape(slab * ZC, NY), modes_prev.reshape(slab * ZC, NY),
        jnp.asarray(cx), jnp.asarray(cx.T.copy()), jnp.asarray(table(NY)),
    )
    return tuple(o.reshape(slab, ZC, NY) for o in outs)


def solution(mesh):
    placed = (
        P("split", "dom", None),
        P("split", "dom", None),
        P("dom"),
        P("dom"),
        P("dom"),
        P("dom", None),
        P("dom", None),
    )
    return jax.shard_map(
        on_device,
        mesh=mesh,
        in_specs=placed,
        out_specs=(P("split", "dom", None),) * 3,
        check_vma=False,
    )
```

```python
import math

import jax
import jax.numpy as jnp
import numpy as np
from jax import lax
from jax.experimental import pallas as pl
from jax.experimental.pallas import tpu as pltpu
from jax.sharding import PartitionSpec as P

F32 = jnp.float32
HIGH = lax.Precision.HIGH
XN, ZN, SN = 4, 16, 8
NX, NY, ZC = 64, 128, 64
QUARTER = 0.25
ST1, ST2, ST3 = 270.0 / 180.0, -27.0 / 180.0, 2.0 / 180.0
GAIN = [2.0 * (-1.0) ** n / math.factorial(2 * n + 2) for n in range(12)]
HALF_PI_2 = (math.pi / 2) ** 2
PAIRS = [(a, b) for a in range(6) for b in range(a, 6)]
MESH = pl.DeviceIdType.MESH


def dot(a, b):
    return jnp.dot(a, b, precision=HIGH, preferred_element_type=F32)


def dot_nt(a, b):
    return lax.dot_general(a, b, (((1,), (1,)), ((), ())), precision=HIGH, preferred_element_type=F32)


def gain_of(u):
    g = jnp.full(u.shape, GAIN[-1], F32)
    for c in GAIN[-2::-1]:
        g = g * u + c
    return g


def cos_table(k, x, length):
    n = k * (2.0 * x + 1.0)
    period = 4.0 * length
    rest = n - period * jnp.floor(n / period + 0.5)
    w = (math.pi / 2) * (rest / length)
    u = w * w
    scale = jnp.where(k == 0, jnp.sqrt(1.0 / length), jnp.sqrt(2.0 / length))
    return scale * (1.0 - 0.5 * u * gain_of(u))


def iota(shape, dim):
    return lax.broadcasted_iota(jnp.int32, shape, dim).astype(F32)


def low_rows(q1, q2, q3):
    return [ST1 * q1 + ST2 * q2 + ST3 * q3, ST2 * q1 + ST3 * q2, ST3 * q1]


def rows(i, n=ZC):
    return pl.ds(pl.multiple_of(i * n, n), n)


NEAR = sorted([(i, d) for i in range(XN) for d in range(-2, 3)], key=lambda p: min(p[0], XN - p[0]) + abs(p[1]))


def kernel(
    ext, low, upp, xs_, ys_, m0_, m1_, cx_, cxt_, cy_,
    nxt, cur, out, ztt,
    xs, ys, m0, m1, cx, cxt, cy,
    rt, rtt, w2, rtb, mz, b1, gn, h0, base2, sscr, kscr, kt, sb, st, nb, near, sel, far, ab, xab, yab, g, hs, hb, e1, ge, yo, yr,
    in_s, nb_s, nb_r, near_s, near_r, far_s, far_r, ab_s, ab_r, h_s, h_r, y_s, y_r,
):
    dom, me = lax.axis_index("dom"), lax.axis_index("split")
    px, pz = dom // ZN, lax.rem(dom, ZN)

    loads = [
        pltpu.make_async_copy(a, b, in_s.at[n])
        for n, (a, b) in enumerate(
            [(m0_, m0), (xs_, xs), (ys_, ys), (cx_, cx), (cy_, cy), (m1_, m1), (cxt_, cxt)]
        )
    ]
    for c in loads:
        c.start()

    def at(dx, dz):
        return lax.rem(px + dx + XN, XN) * ZN + lax.rem(pz + dz + ZN, ZN)

    def other(t):
        return lax.rem(me + t, SN)

    barrier = pltpu.get_barrier_semaphore()

    def greet(d, s):
        pl.semaphore_signal(barrier, inc=1, device_id=(d, s), device_id_type=MESH)

    for k in (2, 1, 3):
        greet(at(0, 4 * k), me)
    for i, d in NEAR[:0:-1]:
        greet(at(i, d), me)
    for t in range(1, SN):
        greet(dom, other(t))

    started = []

    def send(src, dst, ss, rs, d, s):
        c = pltpu.make_async_remote_copy(
            src_ref=src, dst_ref=dst, send_sem=ss, recv_sem=rs, device_id=(d, s), device_id_type=MESH
        )
        c.start()
        started.append(c)

    def arrived(dst, ss, rs):
        pltpu.make_async_remote_copy(
            src_ref=dst, dst_ref=dst, send_sem=ss, recv_sem=rs, device_id=(dom, me), device_id_type=MESH
        ).wait_recv()

    length = ext[0].astype(F32)

    def row_of(r):
        return jnp.where(r < 3, r, r + (length - 6.0))

    k8, r8 = iota((8, ZC), 1), iota((8, ZC), 0)
    rtt[...] = jnp.where((k8 < length) & (r8 < 6), cos_table(k8, row_of(r8), jnp.full((8, ZC), length)), 0.0)
    loads[0].wait()
    for i in range(8):
        sscr[i * 8 : i * 8 + 8, :] = dot(rtt[...], m0[i * ZC : (i + 1) * ZC, :])
    for r in range(6):
        st[0, r] = sscr[pl.ds(r, 8, stride=8), :]
    lowf, uppf = low[0].astype(F32), upp[0].astype(F32)
    nb[0, 0] = jnp.full((8, 128), lowf)
    nb[0, 1] = jnp.full((8, 128), uppf)
    pl.semaphore_wait(barrier, len(NEAR) - 1 + 3 + SN - 1)

    def half(d):
        return slice(3, 6) if d == 2 else slice(0, 3) if d == -2 else slice(0, 6)

    def send_near(step):
        for n in range(len(NEAR) - 1, 0, -1):
            i, d = NEAR[n]
            h = half(d)
            send(st.at[step, h], near.at[step, n, h], near_s.at[step, n], near_r.at[step, n], at(i, d), me)

    send_near(0)
    for k in range(1, 4):
        send(nb.at[0], nb.at[k], nb_s.at[k], nb_r.at[k], at(0, -4 * k), me)

    for c in loads[1:5]:
        c.wait()

    for f in range(2):
        for c, n, move, is_x in ((cy, NY, ys[0, f], False), (cx, NX, xs[0, f], True)):
            move = move.astype(F32)
            row, col = iota((n, n), 0), iota((n, n), 1)
            put = (col == row + move).astype(F32)
            tab = c[...]
            seen = ((col + move >= 0) & (col + move < n)).astype(F32)
            moved = dot(tab, put)
            b = dot_nt(tab * seen, tab)
            if is_x:
                has = jnp.where(jnp.full((n, n), uppf if f else lowf) >= 0, QUARTER, 0.0)
                xab[f, :, 0:NX] = dot_nt(moved, tab) * has
                xab[f, :, NX : 2 * NX] = -b * has
            else:
                yab[f, 0] = dot_nt(tab, moved)
                yab[f, 1] = b

    def put_ab(step, w, lo, up):
        ab[step, w, me, 0:3] = dot(jnp.concatenate(lo, axis=0), yab[0, w]).reshape(3, 8, NY)
        ab[step, w, me, 3:6] = dot(jnp.concatenate(up, axis=0), yab[1, w]).reshape(3, 8, NY)
        for t in range(1, SN):
            send(ab.at[step, w, me], ab.at[step, w, me], ab_s.at[step, w, t], ab_r.at[step, w, t], dom, other(t))

    def own_part(step):
        p = [st[step, r] for r in range(6)]
        put_ab(step, 1, low_rows(p[0], p[1], p[2]), low_rows(p[5], p[4], p[3])[::-1])

    def to_far(step):
        lo = [[jnp.zeros((8, NY), F32)] * 3 for _ in range(4)]
        up = [[jnp.zeros((8, NY), F32)] * 3 for _ in range(4)]
        for n, (i, d) in enumerate(NEAR):
            if n == 0:
                block = st.at[step]
            else:
                h = half(d)
                arrived(near.at[step, n, h], near_s.at[step, n], near_r.at[step, n])
                block = near.at[step, n]
            who = at(-i, -d).astype(F32)
            if d >= -1:
                b = [block[r] for r in range(3, 6)]
                for k in range(4):
                    hit = nb[k, 0] == who
                    lo[k] = [jnp.where(hit, v, a) for v, a in zip(b, lo[k])]
            if d <= 1:
                b = [block[r] for r in range(3)]
                for k in range(4):
                    hit = nb[k, 1] == who
                    up[k] = [jnp.where(hit, v, a) for v, a in zip(b, up[k])]
        for k in (2, 1, 3, 0):
            for r in range(3):
                sel[step, k, r] = lo[k][r]
                sel[step, k, r + 3] = up[k][r]
            if k:
                send(sel.at[step, k], far.at[step, k], far_s.at[step, k], far_r.at[step, k], at(0, 4 * k), me)

    def from_far(step):
        q = [sel[step, 0, r] for r in range(6)]
        for k in (1, 3, 2):
            arrived(far.at[step, k], far_s.at[step, k], far_r.at[step, k])
            q = [a + far[step, k, r] for r, a in enumerate(q)]
        put_ab(step, 0, low_rows(q[2], q[1], q[0]), low_rows(q[3], q[4], q[5])[::-1])

    def gathered(step):
        for w in (1, 0):
            for t in range(1, SN):
                arrived(ab.at[step, w, other(SN - t)], ab_s.at[step, w, t], ab_r.at[step, w, t])

    def sources(step, r):
        return jnp.concatenate([ab[step, w, :, r].reshape(NX, NY) for w in range(2)], axis=0)

    def whole(step):
        for r in range(6):
            g[step, r * NX : (r + 1) * NX, :] = dot(xab[r // 3], sources(step, r))
        g[step, 6 * NX :, :] = jnp.zeros((2 * NX, NY), F32)

    def forced(step, i):
        return gn[rows(i), :] * dot(rt[...], g[step, pl.ds(me * 8 + i, 8, stride=NX), :])

    own_part(0)

    kz = iota((ZC, NY), 0)
    live = kz < length
    lv = jnp.full((ZC, NY), length)
    flat = kz / lv
    flat = flat * flat + (iota((ZC, NY), 1) / NY) ** 2

    def twice(i):
        kx = (me * 8 + i).astype(F32) / NX
        return HALF_PI_2 * (flat + kx * kx)

    loads[5].wait()

    def bases(i, _):
        u = twice(i)
        gain = gain_of(u)
        tw = 2.0 - u * gain
        m = jnp.where(live, m0[rows(i), :], 0.0)
        base = tw * m - jnp.where(live, m1[rows(i), :], 0.0)
        mz[rows(i), :] = m
        gn[rows(i), :] = gain
        b1[rows(i), :] = base
        h0[rows(i), :] = tw * base - m
        return 0

    lax.fori_loop(0, 8, bases, 0)
    for k in range(1, 4):
        arrived(nb.at[k], nb_s.at[k], nb_r.at[k])
    to_far(0)

    for n, (a, b) in enumerate(PAIRS):
        w2[n : n + 1, :] = rtt[a : a + 1, :] * rtt[b : b + 1, :]
    w2[21:24, :] = jnp.zeros((3, ZC), F32)

    def strips(i, _):
        sscr[rows(i, 8), :] = dot(rtt[...], b1[rows(i), :])
        kscr[rows(i, 24), :] = dot(w2[...], gn[rows(i), :])
        return 0

    lax.fori_loop(0, 8, strips, 0)
    for r in range(6):
        sb[r] = sscr[pl.ds(r, 8, stride=8), :]
    for n in range(21):
        kt[n] = kscr[pl.ds(n, 8, stride=24), :]

    def turn(k, _):
        hs[k] = h0[pl.ds(k, 8, stride=ZC), :]
        return 0

    lax.fori_loop(0, ZC, turn, 0, unroll=8)
    for t in range(1, SN):
        dst = pl.multiple_of(other(t) * 8, 8)
        send(hs.at[pl.ds(dst, 8)], hb.at[me], h_s.at[t], h_r.at[t], dom, other(t))
    hb[me] = hs[rows(me, 8)]
    from_far(0)

    k8, r8 = iota((ZC, 8), 0), iota((ZC, 8), 1)
    rt[...] = jnp.where((k8 < length) & (r8 < 6), cos_table(k8, row_of(r8), jnp.full((ZC, 8), length)), 0.0)
    kk, zz = iota((ZC, ZC), 1), iota((ZC, ZC), 0)
    ztt[...] = jnp.where((kk < length) & (zz < length), cos_table(kk, zz, jnp.full((ZC, ZC), length)), 0.0)
    for j in range(8):
        c = rt[pl.ds(me * 8 + j, 1), :]
        for r in range(6):
            rtb[j * 8 + r : j * 8 + r + 1, :] = jnp.broadcast_to(c[:, r : r + 1], (1, NY))
    gathered(0)

    mine = [xab[f, rows(me, 8), :] for f in range(2)]
    g1 = [dot(mine[r // 3], sources(0, r)) for r in range(6)]
    for r in range(6):
        s = sb[r]
        for q in range(6):
            s = s + kt[PAIRS.index((min(r, q), max(r, q)))] * g1[q]
        st[1, r] = s
    send_near(1)
    own_part(1)
    whole(0)

    for t in range(1, SN):
        arrived(hb.at[other(SN - t)], h_s.at[t], h_r.at[t])
    kx2 = (iota((NX, NY), 0) / NX) ** 2 + (iota((NX, NY), 1) / NY) ** 2

    def rowsum(step, j):
        total = rtb[pl.ds(j * 8, 1), :] * g[step, 0:NX, :]
        for r in range(1, 6):
            total = total + rtb[pl.ds(j * 8 + r, 1), :] * g[step, r * NX : (r + 1) * NX, :]
        return total

    def early(j, _):
        z = jnp.full((NX, NY), (me * 8 + j).astype(F32)) / lv
        u = HALF_PI_2 * (kx2 + z * z)
        gain = gain_of(u)
        ge[j] = gain
        e1[j] = hb[:, j].reshape(NX, NY) + gain * (2.0 - u * gain) * rowsum(0, j)
        return 0

    lax.fori_loop(0, 8, early, 0)
    to_far(1)

    def step_one(i, _):
        m = b1[rows(i), :] + forced(0, i)
        cur[rows(i), :] = m
        base2[rows(i), :] = (2.0 - twice(i) * gn[rows(i), :]) * m - mz[rows(i), :]
        return 0

    lax.fori_loop(0, 8, step_one, 0)
    loads[6].wait()
    from_far(1)
    gathered(1)
    whole(1)

    for half_j in range(2):
        js = range(half_j * 4, half_j * 4 + 4)
        e = jnp.concatenate([e1[j] + ge[j] * rowsum(1, j) for j in js], axis=1)
        x = dot(cxt[...], e)
        for n, j in enumerate(js):
            yo[half_j, :, n] = x[:, n * NY : (n + 1) * NY].reshape(SN, 8, NY)
        for t in range(1, SN):
            send(yo.at[half_j, other(t)], yr.at[me, rows(half_j, 4)], y_s.at[half_j, t], y_r.at[half_j, t], dom, other(t))

    def step_two(i, _):
        nxt[rows(i), :] = base2[rows(i), :] + forced(1, i)
        return 0

    lax.fori_loop(0, 8, step_two, 0)
    out[me, 0:4] = yo[0, me]
    out[me, 4:8] = yo[1, me]
    for half_j in range(2):
        for t in range(1, SN):
            src = other(SN - t)
            part = rows(half_j, 4)
            arrived(yr.at[src, part], y_s.at[half_j, t], y_r.at[half_j, t])
            out[src, half_j * 4 : half_j * 4 + 4] = yr[src, half_j * 4 : half_j * 4 + 4]

    for c in started:
        c.wait_send()


def finish(nxt_, cur_, y, ztt, cy, nxt, cur, prs, p, sems):
    copies = [pltpu.make_async_copy(nxt_, nxt, sems.at[0]), pltpu.make_async_copy(cur_, cur, sems.at[1])]
    for c in copies:
        c.start()
    for h in range(2):
        a = dot(ztt[...], jnp.concatenate([y[:, :, i].reshape(ZC, NY) for i in range(h * 4, h * 4 + 4)], axis=1))
        a = jnp.concatenate([a[:, n * NY : (n + 1) * NY] for n in range(4)], axis=0)
        p[h * 4 * ZC : (h + 1) * 4 * ZC, :] = dot(a, cy[...])
        c = pltpu.make_async_copy(p.at[rows(h, 4 * ZC)], prs.at[rows(h, 4 * ZC)], sems.at[2 + h])
        c.start()
        copies.append(c)
    for c in copies:
        c.wait()


def table(n):
    k, x = np.arange(n)[:, None], np.arange(n)[None, :]
    return (np.where(k == 0, math.sqrt(1 / n), math.sqrt(2 / n)) * np.cos(math.pi * k * (x + 0.5) / n)).astype(np.float32)


def on_device(modes_now, modes_prev, z_extent, lower_nbr, upper_nbr, x_shift, y_shift):
    slab = modes_now.shape[0]
    flat = jax.ShapeDtypeStruct((slab * ZC, NY), F32)
    cx, cy = table(NX), jnp.asarray(table(NY))
    hbm, vmem = pl.BlockSpec(memory_space=pltpu.HBM), pl.BlockSpec(memory_space=pltpu.VMEM)
    v = lambda *s: pltpu.VMEM(s, F32)
    sm = lambda *s: pltpu.SMEM(s, jnp.int32)
    dma = pltpu.SemaphoreType.DMA
    nxt, cur, y, ztt = pl.pallas_call(
        kernel,
        out_shape=(flat, flat, jax.ShapeDtypeStruct((8, 8, 8, NY), F32), jax.ShapeDtypeStruct((ZC, ZC), F32)),
        in_specs=[pl.BlockSpec(memory_space=pltpu.SMEM)] * 3 + [hbm] * 7,
        out_specs=(vmem,) * 4,
        scratch_shapes=[
            sm(1, 2), sm(1, 2), v(512, NY), v(512, NY), v(NX, NX), v(NX, NX), v(NY, NY),
            v(ZC, 8), v(8, ZC), v(24, ZC), v(64, NY), v(512, NY), v(512, NY), v(512, NY), v(512, NY), v(512, NY),
            v(64, NY), v(192, NY), v(21, 8, NY), v(6, 8, NY),
            v(2, 6, 8, NY), v(4, 2, 8, NY), v(2, 20, 6, 8, NY), v(2, 4, 6, 8, NY), v(2, 4, 6, 8, NY),
            v(2, 2, 8, 6, 8, NY), v(2, NX, 2 * NX), v(2, 2, NY, NY), v(2, 8 * NX, NY),
            v(ZC, 8, NY), v(8, 8, 8, NY), v(8, NX, NY), v(8, NX, NY), v(2, 8, 4, 8, NY), v(8, 8, 8, NY),
            dma((7,)), dma((4,)), dma((4,)), dma((2, 20)), dma((2, 20)), dma((2, 4)), dma((2, 4)),
            dma((2, 2, 8)), dma((2, 2, 8)), dma((8,)), dma((8,)), dma((2, 8)), dma((2, 8)),
        ],
        compiler_params=pltpu.CompilerParams(collective_id=0, has_side_effects=True, vmem_limit_bytes=20 * 2**20),
    )(z_extent, lower_nbr, upper_nbr, *[
        pltpu.with_memory_space_constraint(a, pltpu.HBM)
        for a in (
            x_shift, y_shift,
            modes_now.reshape(slab * ZC, NY), modes_prev.reshape(slab * ZC, NY),
            jnp.asarray(cx), jnp.asarray(cx.T.copy()), cy,
        )
    ])
    anyw = pl.BlockSpec(memory_space=pl.ANY)
    outs = pl.pallas_call(
        finish,
        out_shape=(flat,) * 3,
        in_specs=[anyw, anyw, vmem, vmem, vmem],
        out_specs=(hbm,) * 3,
        scratch_shapes=[v(512, NY), dma((4,))],
        compiler_params=pltpu.CompilerParams(vmem_limit_bytes=8 * 2**20),
    )(nxt, cur, y, ztt, cy)
    return tuple(o.reshape(slab, ZC, NY) for o in outs)


def solution(mesh):
    placed = (
        P("split", "dom", None),
        P("split", "dom", None),
        P("dom"),
        P("dom"),
        P("dom"),
        P("dom", None),
        P("dom", None),
    )
    return jax.shard_map(
        on_device,
        mesh=mesh,
        in_specs=placed,
        out_specs=(P("split", "dom", None),) * 3,
        check_vma=False,
    )
```

```python
import math

import jax
import jax.numpy as jnp
import numpy as np
from jax import lax
from jax.experimental import pallas as pl
from jax.experimental.pallas import tpu as pltpu
from jax.sharding import PartitionSpec as P

F32 = jnp.float32
HIGH = lax.Precision.HIGH
XN, ZN, SN = 4, 16, 8
NX, NY, ZC = 64, 128, 64
QUARTER = 0.25
ST1, ST2, ST3 = 270.0 / 180.0, -27.0 / 180.0, 2.0 / 180.0
GAIN = [2.0 * (-1.0) ** n / math.factorial(2 * n + 2) for n in range(12)]
HALF_PI_2 = (math.pi / 2) ** 2
PAIRS = [(a, b) for a in range(6) for b in range(a, 6)]
MESH = pl.DeviceIdType.MESH


def dot(a, b):
    return jnp.dot(a, b, precision=HIGH, preferred_element_type=F32)


def dot_nt(a, b):
    return lax.dot_general(a, b, (((1,), (1,)), ((), ())), precision=HIGH, preferred_element_type=F32)


def gain_of(u):
    g = jnp.full(u.shape, GAIN[-1], F32)
    for c in GAIN[-2::-1]:
        g = g * u + c
    return g


def cos_table(k, x, length):
    n = k * (2.0 * x + 1.0)
    period = 4.0 * length
    rest = n - period * jnp.floor(n / period + 0.5)
    w = (math.pi / 2) * (rest / length)
    u = w * w
    scale = jnp.where(k == 0, jnp.sqrt(1.0 / length), jnp.sqrt(2.0 / length))
    return scale * (1.0 - 0.5 * u * gain_of(u))


def iota(shape, dim):
    return lax.broadcasted_iota(jnp.int32, shape, dim).astype(F32)


def low_rows(q1, q2, q3):
    return [ST1 * q1 + ST2 * q2 + ST3 * q3, ST2 * q1 + ST3 * q2, ST3 * q1]


def rows(i, n=ZC):
    return pl.ds(pl.multiple_of(i * n, n), n)


WINDOWS = [
    sorted([(i, d) for i in range(XN) for d in ds], key=lambda p: min(p[0], XN - p[0]) + abs(p[1]))
    for ds in (range(-1, 3), range(-2, 2))
]
GREET = [(i, d) for d in (-2, 2, -1, 1, 0) for i in (2, 1, 3, 0) if (i, d) != (0, 0)]
KH = ZC // 2


def kernel(
    ext, low, upp, xs_, ys_, m0_, m1_, cx_, cxt_, cy_,
    nxt, cur, out, ztt,
    xs, ys, m0, m1, cx, cxt, cy,
    rt, rtt, w2, rtb, mz, b1, gn, h0, base2, sscr, kscr, kt, sb, st, nb, near, sel, far, aa, bb, xa, xb, yab, gb, g,
    hs, hb, e1, ge, yo, yr,
    in_s, nb_s, nb_r, near_s, near_r, far_s, far_r, aa_s, aa_r, bb_s, bb_r, h_s, h_r, y_s, y_r,
):
    dom, me = lax.axis_index("dom"), lax.axis_index("split")
    px, pz = dom // ZN, lax.rem(dom, ZN)
    chip, core = me // 2, lax.rem(me, 2)

    loads = [
        pltpu.make_async_copy(a, b, in_s.at[n])
        for n, (a, b) in enumerate([(m0_, m0), (xs_, xs), (ys_, ys), (cx_, cx), (cy_, cy), (m1_, m1), (cxt_, cxt)])
    ]
    for c in loads:
        c.start()

    def at(dx, dz):
        return lax.rem(px + dx + XN, XN) * ZN + lax.rem(pz + dz + ZN, ZN)

    def other(t):
        return lax.rem(me + t, SN)

    barrier = pltpu.get_barrier_semaphore()

    def greet(d, s):
        pl.semaphore_signal(barrier, inc=1, device_id=(d, s), device_id_type=MESH)

    for k in (2, 1, 3):
        greet(at(0, 4 * k), me)
    for i, d in GREET:
        greet(at(i, d), me)
    for t in range(1, SN):
        greet(dom, other(t))

    started = []

    def send(src, dst, ss, rs, d, s):
        c = pltpu.make_async_remote_copy(
            src_ref=src, dst_ref=dst, send_sem=ss, recv_sem=rs, device_id=(d, s), device_id_type=MESH
        )
        c.start()
        started.append(c)

    def arrived(dst, ss, rs):
        pltpu.make_async_remote_copy(
            src_ref=dst, dst_ref=dst, send_sem=ss, recv_sem=rs, device_id=(dom, me), device_id_type=MESH
        ).wait_recv()

    length = ext[0].astype(F32)

    def row_of(r):
        return jnp.where(r < 3, r, r + (length - 6.0))

    def row_table(k, r):
        return jnp.where((k < length) & (r < 6), cos_table(k, row_of(r), jnp.full(k.shape, length)), 0.0)

    rtt[...] = row_table(iota((8, ZC), 1), iota((8, ZC), 0))
    lowf, uppf = low[0].astype(F32), upp[0].astype(F32)
    nb[0, 0] = jnp.full((8, 128), lowf)
    nb[0, 1] = jnp.full((8, 128), uppf)
    loads[0].wait()
    for i in range(8):
        sscr[i * 8 : i * 8 + 8, :] = dot(rtt[...], m0[i * ZC : (i + 1) * ZC, :])
    for r in range(6):
        st[0, r] = sscr[pl.ds(r, 8, stride=8), :]
    pl.semaphore_wait(barrier, len(GREET) + 3 + SN - 1)

    def strip_rows(f):
        return slice(3, 6) if f == 0 else slice(0, 3)

    def send_near(step):
        for f in range(2):
            for n in range(15, 0, -1):
                i, d = WINDOWS[f][n]
                send(
                    st.at[step, strip_rows(f)], near.at[step, f, n],
                    near_s.at[step, f, n], near_r.at[step, f, n], at(i, d), me,
                )

    for k in (2, 1, 3):
        send(nb.at[0], nb.at[k], nb_s.at[k], nb_r.at[k], at(0, -4 * k), me)
    send_near(0)

    for c in loads[1:5]:
        c.wait()

    for f in range(2):
        for c, n, move, is_x in ((cy, NY, ys[0, f], False), (cx, NX, xs[0, f], True)):
            move = move.astype(F32)
            row, col = iota((n, n), 0), iota((n, n), 1)
            put = (col == row + move).astype(F32)
            tab = c[...]
            seen = ((col + move >= 0) & (col + move < n)).astype(F32)
            moved = dot(tab, put)
            b = dot_nt(tab * seen, tab)
            if is_x:
                has = jnp.where(jnp.full((n, n), uppf if f else lowf) >= 0, QUARTER, 0.0)
                xa[f] = dot_nt(moved, tab) * has
                xb[f] = -b * has
            else:
                yab[f, 0] = dot_nt(tab, moved)
                yab[f, 1] = b

    def own_part(step):
        p = [st[step, r] for r in range(6)]
        for f, part in enumerate((low_rows(p[0], p[1], p[2]), low_rows(p[5], p[4], p[3])[::-1])):
            bb[step, me, 3 * f : 3 * f + 3] = dot(jnp.concatenate(part, axis=0), yab[f, 1]).reshape(3, 8, NY)
        for t in range(1, SN):
            send(bb.at[step, me], bb.at[step, me], bb_s.at[step, t], bb_r.at[step, t], dom, other(t))

    def to_far(step, f):
        acc = [[jnp.zeros((8, NY), F32)] * 3 for _ in range(4)]
        rows_f = strip_rows(f)
        for n, (i, d) in enumerate(WINDOWS[f]):
            if n == 0:
                block = [st[step, r] for r in range(rows_f.start, rows_f.stop)]
            else:
                arrived(near.at[step, f, n], near_s.at[step, f, n], near_r.at[step, f, n])
                block = [near[step, f, n, r] for r in range(3)]
            who = at(-i, -d).astype(F32)
            for k in range(4):
                hit = nb[k, f] == who
                acc[k] = [jnp.where(hit, v, a) for v, a in zip(block, acc[k])]
        for k in (2, 1, 3, 0):
            for r in range(3):
                sel[step, f, k, r] = acc[k][r]
            if k:
                send(
                    sel.at[step, f, k], far.at[step, f, k],
                    far_s.at[step, f, k], far_r.at[step, f, k], at(0, 4 * k), me,
                )

    def from_far(step, f):
        q = [sel[step, f, 0, r] for r in range(3)]
        for k in (1, 3, 2):
            arrived(far.at[step, f, k], far_s.at[step, f, k], far_r.at[step, f, k])
            q = [a + far[step, f, k, r] for r, a in enumerate(q)]
        part = low_rows(*q)[::-1] if f else low_rows(*q[::-1])
        aa[step, f, me] = dot(jnp.concatenate(part, axis=0), yab[f, 0]).reshape(3, 8, NY)
        for t in range(1, SN):
            send(aa.at[step, f, me], aa.at[step, f, me], aa_s.at[step, f, t], aa_r.at[step, f, t], dom, other(t))

    def gathered_own(step):
        for t in range(1, SN):
            arrived(bb.at[step, other(SN - t)], bb_s.at[step, t], bb_r.at[step, t])

    def gathered(step, f):
        for t in range(1, SN):
            arrived(aa.at[step, f, other(SN - t)], aa_s.at[step, f, t], aa_r.at[step, f, t])

    def theirs(step, r):
        return aa[step, r // 3, :, r % 3].reshape(NX, NY)

    def ours(step, r):
        return bb[step, :, r].reshape(NX, NY)

    def forced(step, i):
        return gn[rows(i), :] * dot(rt[...], g[step, pl.ds(me * 8 + i, 8, stride=NX), :])

    own_part(0)

    kz = iota((ZC, NY), 0)
    live = kz < length
    lv = jnp.full((ZC, NY), length)
    flat = kz / lv
    flat = flat * flat + (iota((ZC, NY), 1) / NY) ** 2

    def twice(i):
        kx = (me * 8 + i).astype(F32) / NX
        return HALF_PI_2 * (flat + kx * kx)

    loads[5].wait()

    def bases(i, _):
        u = twice(i)
        gain = gain_of(u)
        tw = 2.0 - u * gain
        m = jnp.where(live, m0[rows(i), :], 0.0)
        base = tw * m - jnp.where(live, m1[rows(i), :], 0.0)
        mz[rows(i), :] = m
        gn[rows(i), :] = gain
        b1[rows(i), :] = base
        h0[rows(i), :] = tw * base - m
        return 0

    lax.fori_loop(0, 8, bases, 0)
    for k in (1, 3, 2):
        arrived(nb.at[k], nb_s.at[k], nb_r.at[k])
    to_far(0, 0)
    to_far(0, 1)

    def turn(k, _):
        hs[k] = h0[pl.ds(k, 8, stride=ZC), :]
        return 0

    lax.fori_loop(0, ZC, turn, 0, unroll=8)

    def send_h(part):
        for t in range(1, SN):
            first = pl.multiple_of(lax.rem(other(t), 2) * KH + part * 16, 16)
            send(
                hs.at[pl.ds(first, 16)], hb.at[me, rows(part, 16)], h_s.at[part, t], h_r.at[part, t], dom, other(t)
            )

    send_h(0)
    hb[me] = hs[rows(core, KH)]
    for n, (a, b) in enumerate(PAIRS):
        w2[n : n + 1, :] = rtt[a : a + 1, :] * rtt[b : b + 1, :]
    w2[21:24, :] = jnp.zeros((3, ZC), F32)

    def strips(i, _):
        sscr[rows(i, 8), :] = dot(rtt[...], b1[rows(i), :])
        kscr[rows(i, 24), :] = dot(w2[...], gn[rows(i), :])
        return 0

    lax.fori_loop(0, 8, strips, 0)
    for r in range(6):
        sb[r] = sscr[pl.ds(r, 8, stride=8), :]
    for n in range(21):
        kt[n] = kscr[pl.ds(n, 8, stride=24), :]
    gathered_own(0)
    for r in range(6):
        gb[r] = dot(xb[r // 3, rows(me, 8), :], ours(0, r))
    from_far(0, 0)
    from_far(0, 1)

    rt[...] = row_table(iota((ZC, 8), 0), iota((ZC, 8), 1))
    kk, zz = iota((ZC, ZC), 1), iota((ZC, ZC), 0)
    ztt[...] = jnp.where((kk < length) & (zz < length), cos_table(kk, zz, jnp.full((ZC, ZC), length)), 0.0)
    g1 = []
    for f in range(2):
        gathered(0, f)
        for r in range(3 * f, 3 * f + 3):
            g1.append(gb[r] + dot(xa[f, rows(me, 8), :], theirs(0, r)))
    for r in range(6):
        s = sb[r]
        for q in range(6):
            s = s + kt[PAIRS.index((min(r, q), max(r, q)))] * g1[q]
        st[1, r] = s
    send_near(1)
    own_part(1)
    send_h(1)
    for step in range(2):
        g[step, 6 * NX :, :] = jnp.zeros((2 * NX, NY), F32)
    for r in range(6):
        g[0, r * NX : (r + 1) * NX, :] = dot(xb[r // 3], ours(0, r)) + dot(xa[r // 3], theirs(0, r))
    shape = (KH, 8, NY)
    rtb[...] = row_table(iota(shape, 0) + (core * KH).astype(F32), iota(shape, 1))

    kx2 = (iota((NX, NY), 0) / NX) ** 2 + (iota((NX, NY), 1) / NY) ** 2

    def early(j, _):
        z = jnp.full((NX, NY), (core * KH + j).astype(F32)) / lv
        u = HALF_PI_2 * (kx2 + z * z)
        gain = gain_of(u)
        total = rtb[j, 0:1, :] * g[0, 0:NX, :]
        for r in range(1, 6):
            total = total + rtb[j, r : r + 1, :] * g[0, r * NX : (r + 1) * NX, :]
        ge[j] = gain
        e1[j] = hb[:, j].reshape(NX, NY) + gain * (2.0 - u * gain) * total
        return 0

    def arrived_h(part):
        for t in range(1, SN):
            arrived(hb.at[other(SN - t), rows(part, 16)], h_s.at[part, t], h_r.at[part, t])

    arrived_h(0)
    lax.fori_loop(0, 16, early, 0)
    to_far(1, 0)
    to_far(1, 1)

    def step_one(i, _):
        m = b1[rows(i), :] + forced(0, i)
        cur[rows(i), :] = m
        base2[rows(i), :] = (2.0 - twice(i) * gn[rows(i), :]) * m - mz[rows(i), :]
        return 0

    gathered_own(1)
    for r in range(6):
        g[1, r * NX : (r + 1) * NX, :] = dot(xb[r // 3], ours(1, r))
    arrived_h(1)
    lax.fori_loop(16, KH, early, 0)
    loads[6].wait()
    from_far(1, 0)
    from_far(1, 1)
    lax.fori_loop(0, 8, step_one, 0)
    for f in range(2):
        gathered(1, f)
        for r in range(3 * f, 3 * f + 3):
            g[1, r * NX : (r + 1) * NX, :] += dot(xa[f], theirs(1, r))

    twin = 1 - core
    cx16 = cxt[rows(chip, 16), :]
    for part in range(4):
        parts = []
        for j in range(part * 8, part * 8 + 8, 2):
            weights = [[jnp.broadcast_to(rtb[jj, r : r + 1, :], (8, NY)) for r in range(6)] for jj in (j, j + 1)]
            tiles = [[], []]
            for x in range(8):
                src = [g[1, r * NX + x * 8 : r * NX + x * 8 + 8, :] for r in range(6)]
                for n in range(2):
                    total = weights[n][0] * src[0]
                    for r in range(1, 6):
                        total = total + weights[n][r] * src[r]
                    at_x = slice(x * 8, x * 8 + 8)
                    tiles[n].append(e1[j + n, at_x, :] + ge[j + n, at_x, :] * total)
            parts += [jnp.concatenate(t, axis=0) for t in tiles]
        x = dot(cx16, jnp.concatenate(parts, axis=1))
        for c in range(2):
            for j in range(8):
                yo[c, part * 8 + j] = x[c * 8 : c * 8 + 8, j * NY : (j + 1) * NY]
        p8 = rows(part, 8)
        send(yo.at[twin, p8], yr.at[p8], y_s.at[part], y_r.at[part], dom, chip * 2 + twin)

    def step_two(i, _):
        nxt[rows(i), :] = base2[rows(i), :] + forced(1, i)
        return 0

    lax.fori_loop(0, 8, step_two, 0)
    out[core] = yo[core]
    for part in range(4):
        p8 = rows(part, 8)
        arrived(yr.at[p8], y_s.at[part], y_r.at[part])
        out[twin, p8] = yr[p8]

    for c in started:
        c.wait_send()


def finish(nxt_, cur_, y, ztt, cy, nxt, cur, prs, p, sems):
    copies = [pltpu.make_async_copy(nxt_, nxt, sems.at[0]), pltpu.make_async_copy(cur_, cur, sems.at[1])]
    for c in copies:
        c.start()
    for h in range(2):
        a = dot(ztt[...], jnp.concatenate([y[:, :, i].reshape(ZC, NY) for i in range(h * 4, h * 4 + 4)], axis=1))
        a = jnp.concatenate([a[:, n * NY : (n + 1) * NY] for n in range(4)], axis=0)
        p[h * 4 * ZC : (h + 1) * 4 * ZC, :] = dot(a, cy[...])
        c = pltpu.make_async_copy(p.at[rows(h, 4 * ZC)], prs.at[rows(h, 4 * ZC)], sems.at[2 + h])
        c.start()
        copies.append(c)
    for c in copies:
        c.wait()


def table(n):
    k, x = np.arange(n)[:, None], np.arange(n)[None, :]
    return (np.where(k == 0, math.sqrt(1 / n), math.sqrt(2 / n)) * np.cos(math.pi * k * (x + 0.5) / n)).astype(np.float32)


def on_device(modes_now, modes_prev, z_extent, lower_nbr, upper_nbr, x_shift, y_shift):
    slab = modes_now.shape[0]
    flat = jax.ShapeDtypeStruct((slab * ZC, NY), F32)
    cx, cy = table(NX), jnp.asarray(table(NY))
    hbm, vmem = pl.BlockSpec(memory_space=pltpu.HBM), pl.BlockSpec(memory_space=pltpu.VMEM)
    v = lambda *s: pltpu.VMEM(s, F32)
    sm = lambda *s: pltpu.SMEM(s, jnp.int32)
    dma = pltpu.SemaphoreType.DMA
    nxt, cur, y, ztt = pl.pallas_call(
        kernel,
        out_shape=(flat, flat, jax.ShapeDtypeStruct((2, KH, 8, NY), F32), jax.ShapeDtypeStruct((ZC, ZC), F32)),
        in_specs=[pl.BlockSpec(memory_space=pltpu.SMEM)] * 3 + [hbm] * 7,
        out_specs=(vmem,) * 4,
        scratch_shapes=[
            sm(1, 2), sm(1, 2), v(512, NY), v(512, NY), v(NX, NX), v(NX, NX), v(NY, NY),
            v(ZC, 8), v(8, ZC), v(24, ZC), v(KH, 8, NY), v(512, NY), v(512, NY), v(512, NY), v(512, NY), v(512, NY),
            v(64, NY), v(192, NY), v(21, 8, NY), v(6, 8, NY),
            v(2, 6, 8, NY), v(4, 2, 8, NY), v(2, 2, 16, 3, 8, NY), v(2, 2, 4, 3, 8, NY), v(2, 2, 4, 3, 8, NY),
            v(2, 2, 8, 3, 8, NY), v(2, 8, 6, 8, NY), v(2, NX, NX), v(2, NX, NX), v(2, 2, NY, NY), v(6, 8, NY),
            v(2, 8 * NX, NY),
            v(ZC, 8, NY), v(8, KH, 8, NY), v(KH, NX, NY), v(KH, NX, NY), v(2, KH, 8, NY), v(KH, 8, NY),
            dma((7,)), dma((4,)), dma((4,)), dma((2, 2, 16)), dma((2, 2, 16)), dma((2, 2, 4)), dma((2, 2, 4)),
            dma((2, 2, 8)), dma((2, 2, 8)), dma((2, 8)), dma((2, 8)), dma((2, 8)), dma((2, 8)), dma((4,)), dma((4,)),
        ],
        compiler_params=pltpu.CompilerParams(collective_id=0, has_side_effects=True, vmem_limit_bytes=20 * 2**20),
    )(z_extent, lower_nbr, upper_nbr, *[
        pltpu.with_memory_space_constraint(a, pltpu.HBM)
        for a in (
            x_shift, y_shift,
            modes_now.reshape(slab * ZC, NY), modes_prev.reshape(slab * ZC, NY),
            jnp.asarray(cx), jnp.asarray(cx.T.copy()), cy,
        )
    ])
    anyw = pl.BlockSpec(memory_space=pl.ANY)
    outs = pl.pallas_call(
        finish,
        out_shape=(flat,) * 3,
        in_specs=[anyw, anyw, vmem, vmem, vmem],
        out_specs=(hbm,) * 3,
        scratch_shapes=[v(512, NY), dma((4,))],
        compiler_params=pltpu.CompilerParams(vmem_limit_bytes=8 * 2**20),
    )(nxt, cur, y, ztt, cy)
    return tuple(o.reshape(slab, ZC, NY) for o in outs)


def solution(mesh):
    placed = (
        P("split", "dom", None),
        P("split", "dom", None),
        P("dom"),
        P("dom"),
        P("dom"),
        P("dom", None),
        P("dom", None),
    )
    return jax.shard_map(
        on_device,
        mesh=mesh,
        in_specs=placed,
        out_specs=(P("split", "dom", None),) * 3,
        check_vma=False,
    )
```

```python
import math

import jax
import jax.numpy as jnp
import numpy as np
from jax import lax
from jax.experimental import pallas as pl
from jax.experimental.pallas import tpu as pltpu
from jax.sharding import PartitionSpec as P

F32 = jnp.float32
HIGH = lax.Precision.HIGH
XN, ZN, SN = 4, 16, 8
NX, NY, ZC = 64, 128, 64
QUARTER = 0.25
ST1, ST2, ST3 = 270.0 / 180.0, -27.0 / 180.0, 2.0 / 180.0
GAIN = [2.0 * (-1.0) ** n / math.factorial(2 * n + 2) for n in range(12)]
HALF_PI_2 = (math.pi / 2) ** 2
PAIRS = [(a, b) for a in range(6) for b in range(a, 6)]
MESH = pl.DeviceIdType.MESH


def dot(a, b):
    return jnp.dot(a, b, precision=HIGH, preferred_element_type=F32)


def dot_nt(a, b):
    return lax.dot_general(a, b, (((1,), (1,)), ((), ())), precision=HIGH, preferred_element_type=F32)


def gain_of(u):
    g = jnp.full(u.shape, GAIN[-1], F32)
    for c in GAIN[-2::-1]:
        g = g * u + c
    return g


def cos_table(k, x, length):
    n = k * (2.0 * x + 1.0)
    period = 4.0 * length
    rest = n - period * jnp.floor(n / period + 0.5)
    w = (math.pi / 2) * (rest / length)
    u = w * w
    scale = jnp.where(k == 0, jnp.sqrt(1.0 / length), jnp.sqrt(2.0 / length))
    return scale * (1.0 - 0.5 * u * gain_of(u))


def iota(shape, dim):
    return lax.broadcasted_iota(jnp.int32, shape, dim).astype(F32)


def low_rows(q1, q2, q3):
    return [ST1 * q1 + ST2 * q2 + ST3 * q3, ST2 * q1 + ST3 * q2, ST3 * q1]


def rows(i, n=ZC):
    return pl.ds(pl.multiple_of(i * n, n), n)


WINDOWS = [
    sorted([(i, d) for i in range(XN) for d in ds], key=lambda p: min(p[0], XN - p[0]) + abs(p[1]))
    for ds in (range(-1, 3), range(-2, 2))
]
GREET = [(i, d) for d in (-2, 2, -1, 1, 0) for i in (2, 1, 3, 0) if (i, d) != (0, 0)]
KH = ZC // 2


def kernel(
    ext, low, upp, xs_, ys_, m0_, m1_, cx_, cxt_, cy_,
    nxt, cur, out, ztt,
    xs, ys, m0, m1, cx, cxt, cy,
    rt, rtt, w2, rtb, mz, b1, gn, h0, base2, sscr, kscr, kt, sb, st, nb, near, sel, far, aa, bb, xa, xb, yab, gb, g,
    hs, hb, e1, ge, yo, yr,
    in_s, nb_s, nb_r, near_s, near_r, far_s, far_r, aa_s, aa_r, bb_s, bb_r, h_s, h_r, y_s, y_r,
):
    dom, me = lax.axis_index("dom"), lax.axis_index("split")
    px, pz = dom // ZN, lax.rem(dom, ZN)
    chip, core = me // 2, lax.rem(me, 2)

    loads = [
        pltpu.make_async_copy(a, b, in_s.at[n])
        for n, (a, b) in enumerate([(m0_, m0), (xs_, xs), (ys_, ys), (cx_, cx), (cy_, cy), (m1_, m1), (cxt_, cxt)])
    ]
    for c in loads:
        c.start()

    def at(dx, dz):
        return lax.rem(px + dx + XN, XN) * ZN + lax.rem(pz + dz + ZN, ZN)

    def other(t):
        return lax.rem(me + t, SN)

    barrier = pltpu.get_barrier_semaphore()

    def greet(d, s):
        pl.semaphore_signal(barrier, inc=1, device_id=(d, s), device_id_type=MESH)

    for k in (1, 3):
        greet(at(0, 4 * k), me)
    for i, d in GREET:
        greet(at(i, d), me)
    for t in range(1, SN):
        greet(dom, other(t))

    started = []

    def send(src, dst, ss, rs, d, s):
        c = pltpu.make_async_remote_copy(
            src_ref=src, dst_ref=dst, send_sem=ss, recv_sem=rs, device_id=(d, s), device_id_type=MESH
        )
        c.start()
        started.append(c)

    def arrived(dst, ss, rs):
        pltpu.make_async_remote_copy(
            src_ref=dst, dst_ref=dst, send_sem=ss, recv_sem=rs, device_id=(dom, me), device_id_type=MESH
        ).wait_recv()

    length = ext[0].astype(F32)

    def row_of(r):
        return jnp.where(r < 3, r, r + (length - 6.0))

    def row_table(k, r):
        return jnp.where((k < length) & (r < 6), cos_table(k, row_of(r), jnp.full(k.shape, length)), 0.0)

    rtt[...] = row_table(iota((8, ZC), 1), iota((8, ZC), 0))
    lowf, uppf = low[0].astype(F32), upp[0].astype(F32)
    nb[0, 0] = jnp.full((8, 128), lowf)
    nb[0, 1] = jnp.full((8, 128), uppf)
    loads[0].wait()
    for i in range(8):
        sscr[i * 8 : i * 8 + 8, :] = dot(rtt[...], m0[i * ZC : (i + 1) * ZC, :])
    for r in range(6):
        st[0, r] = sscr[pl.ds(r, 8, stride=8), :]
    pl.semaphore_wait(barrier, len(GREET) + 2 + SN - 1)

    def strip_rows(f):
        return slice(3, 6) if f == 0 else slice(0, 3)

    def send_near(step):
        for f in range(2):
            for n in range(15, 0, -1):
                i, d = WINDOWS[f][n]
                send(
                    st.at[step, strip_rows(f)], near.at[step, f, n],
                    near_s.at[step, f, n], near_r.at[step, f, n], at(i, d), me,
                )

    for k in (1, 3):
        send(nb.at[0], nb.at[k], nb_s.at[k], nb_r.at[k], at(0, -4 * k), me)
    send_near(0)

    for c in loads[1:5]:
        c.wait()

    for f in range(2):
        for c, n, move, is_x in ((cy, NY, ys[0, f], False), (cx, NX, xs[0, f], True)):
            move = move.astype(F32)
            row, col = iota((n, n), 0), iota((n, n), 1)
            put = (col == row + move).astype(F32)
            tab = c[...]
            seen = ((col + move >= 0) & (col + move < n)).astype(F32)
            moved = dot(tab, put)
            b = dot_nt(tab * seen, tab)
            if is_x:
                has = jnp.where(jnp.full((n, n), uppf if f else lowf) >= 0, QUARTER, 0.0)
                xa[f] = dot_nt(moved, tab) * has
                xb[f] = -b * has
            else:
                yab[f, 0] = dot_nt(tab, moved)
                yab[f, 1] = b

    def own_part(step):
        p = [st[step, r] for r in range(6)]
        for f, part in enumerate((low_rows(p[0], p[1], p[2]), low_rows(p[5], p[4], p[3])[::-1])):
            bb[step, me, 3 * f : 3 * f + 3] = dot(jnp.concatenate(part, axis=0), yab[f, 1]).reshape(3, 8, NY)
        for t in range(1, SN):
            send(bb.at[step, me], bb.at[step, me], bb_s.at[step, t], bb_r.at[step, t], dom, other(t))

    def to_far(step, f, ks, wait=True):
        acc = {k: [jnp.zeros((8, NY), F32)] * 3 for k in ks}
        rows_f = strip_rows(f)
        for n, (i, d) in enumerate(WINDOWS[f]):
            if n == 0:
                block = [st[step, r] for r in range(rows_f.start, rows_f.stop)]
            else:
                if wait:
                    arrived(near.at[step, f, n], near_s.at[step, f, n], near_r.at[step, f, n])
                block = [near[step, f, n, r] for r in range(3)]
            who = at(-i, -d).astype(F32)
            for k in ks:
                hit = nb[k, f] == who
                acc[k] = [jnp.where(hit, v, a) for v, a in zip(block, acc[k])]
        for k in ks:
            for r in range(3):
                sel[step, f, k, r] = acc[k][r]
            if k:
                send(
                    sel.at[step, f, k], far.at[step, f, k],
                    far_s.at[step, f, k], far_r.at[step, f, k], at(0, 4 * k), me,
                )

    def from_far(step, f):
        q = [sel[step, f, 0, r] for r in range(3)]
        for k in (1, 3, 2):
            arrived(far.at[step, f, k], far_s.at[step, f, k], far_r.at[step, f, k])
            q = [a + far[step, f, k, r] for r, a in enumerate(q)]
        part = low_rows(*q)[::-1] if f else low_rows(*q[::-1])
        aa[step, f, me] = dot(jnp.concatenate(part, axis=0), yab[f, 0]).reshape(3, 8, NY)
        for t in range(1, SN):
            send(aa.at[step, f, me], aa.at[step, f, me], aa_s.at[step, f, t], aa_r.at[step, f, t], dom, other(t))

    def gathered_own(step):
        for t in range(1, SN):
            arrived(bb.at[step, other(SN - t)], bb_s.at[step, t], bb_r.at[step, t])

    def gathered(step, f):
        for t in range(1, SN):
            arrived(aa.at[step, f, other(SN - t)], aa_s.at[step, f, t], aa_r.at[step, f, t])

    def theirs(step, r):
        return aa[step, r // 3, :, r % 3].reshape(NX, NY)

    def ours(step, r):
        return bb[step, :, r].reshape(NX, NY)

    def forced(step, i):
        return gn[rows(i), :] * dot(rt[...], g[step, pl.ds(me * 8 + i, 8, stride=NX), :])

    own_part(0)

    kz = iota((ZC, NY), 0)
    live = kz < length
    lv = jnp.full((ZC, NY), length)
    flat = kz / lv
    flat = flat * flat + (iota((ZC, NY), 1) / NY) ** 2

    def twice(i):
        kx = (me * 8 + i).astype(F32) / NX
        return HALF_PI_2 * (flat + kx * kx)

    loads[5].wait()

    def bases(i, _):
        u = twice(i)
        gain = gain_of(u)
        tw = 2.0 - u * gain
        m = jnp.where(live, m0[rows(i), :], 0.0)
        base = tw * m - jnp.where(live, m1[rows(i), :], 0.0)
        mz[rows(i), :] = m
        gn[rows(i), :] = gain
        b1[rows(i), :] = base
        h0[rows(i), :] = tw * base - m
        return 0

    lax.fori_loop(0, 8, bases, 0)
    arrived(nb.at[1], nb_s.at[1], nb_r.at[1])
    send(nb.at[1], nb.at[2], nb_s.at[2], nb_r.at[2], at(0, -4), me)
    arrived(nb.at[3], nb_s.at[3], nb_r.at[3])
    to_far(0, 0, (1, 3, 0))
    to_far(0, 1, (1, 3, 0))
    arrived(nb.at[2], nb_s.at[2], nb_r.at[2])
    to_far(0, 0, (2,), False)
    to_far(0, 1, (2,), False)

    def turn(k, _):
        hs[k] = h0[pl.ds(k, 8, stride=ZC), :]
        return 0

    lax.fori_loop(0, ZC, turn, 0, unroll=8)

    def send_h(part):
        for t in range(1, SN):
            first = pl.multiple_of(lax.rem(other(t), 2) * KH + part * 16, 16)
            send(
                hs.at[pl.ds(first, 16)], hb.at[me, rows(part, 16)], h_s.at[part, t], h_r.at[part, t], dom, other(t)
            )

    send_h(0)
    hb[me] = hs[rows(core, KH)]
    for n, (a, b) in enumerate(PAIRS):
        w2[n : n + 1, :] = rtt[a : a + 1, :] * rtt[b : b + 1, :]
    w2[21:24, :] = jnp.zeros((3, ZC), F32)

    def strips(i, _):
        sscr[rows(i, 8), :] = dot(rtt[...], b1[rows(i), :])
        kscr[rows(i, 24), :] = dot(w2[...], gn[rows(i), :])
        return 0

    lax.fori_loop(0, 8, strips, 0)
    for r in range(6):
        sb[r] = sscr[pl.ds(r, 8, stride=8), :]
    for n in range(21):
        kt[n] = kscr[pl.ds(n, 8, stride=24), :]
    gathered_own(0)
    for r in range(6):
        gb[r] = dot(xb[r // 3, rows(me, 8), :], ours(0, r))
    from_far(0, 0)
    from_far(0, 1)

    rt[...] = row_table(iota((ZC, 8), 0), iota((ZC, 8), 1))
    kk, zz = iota((ZC, ZC), 1), iota((ZC, ZC), 0)
    ztt[...] = jnp.where((kk < length) & (zz < length), cos_table(kk, zz, jnp.full((ZC, ZC), length)), 0.0)
    g1 = []
    for f in range(2):
        gathered(0, f)
        for r in range(3 * f, 3 * f + 3):
            g1.append(gb[r] + dot(xa[f, rows(me, 8), :], theirs(0, r)))
    for r in range(6):
        s = sb[r]
        for q in range(6):
            s = s + kt[PAIRS.index((min(r, q), max(r, q)))] * g1[q]
        st[1, r] = s
    send_near(1)
    own_part(1)
    send_h(1)
    for step in range(2):
        g[step, 6 * NX :, :] = jnp.zeros((2 * NX, NY), F32)
    for r in range(6):
        g[0, r * NX : (r + 1) * NX, :] = dot(xb[r // 3], ours(0, r)) + dot(xa[r // 3], theirs(0, r))
    shape = (KH, 8, NY)
    rtb[...] = row_table(iota(shape, 0) + (core * KH).astype(F32), iota(shape, 1))

    kx2 = (iota((NX, NY), 0) / NX) ** 2 + (iota((NX, NY), 1) / NY) ** 2

    def early(j, _):
        z = jnp.full((NX, NY), (core * KH + j).astype(F32)) / lv
        u = HALF_PI_2 * (kx2 + z * z)
        gain = gain_of(u)
        total = rtb[j, 0:1, :] * g[0, 0:NX, :]
        for r in range(1, 6):
            total = total + rtb[j, r : r + 1, :] * g[0, r * NX : (r + 1) * NX, :]
        ge[j] = gain
        e1[j] = hb[:, j].reshape(NX, NY) + gain * (2.0 - u * gain) * total
        return 0

    def arrived_h(part):
        for t in range(1, SN):
            arrived(hb.at[other(SN - t), rows(part, 16)], h_s.at[part, t], h_r.at[part, t])

    arrived_h(0)
    lax.fori_loop(0, 16, early, 0)
    to_far(1, 0, (2, 1, 3, 0))
    to_far(1, 1, (2, 1, 3, 0))

    def step_one(i, _):
        m = b1[rows(i), :] + forced(0, i)
        cur[rows(i), :] = m
        base2[rows(i), :] = (2.0 - twice(i) * gn[rows(i), :]) * m - mz[rows(i), :]
        return 0

    gathered_own(1)
    for r in range(6):
        g[1, r * NX : (r + 1) * NX, :] = dot(xb[r // 3], ours(1, r))
    arrived_h(1)
    lax.fori_loop(16, KH, early, 0)
    loads[6].wait()
    from_far(1, 0)
    from_far(1, 1)
    lax.fori_loop(0, 8, step_one, 0)
    for f in range(2):
        gathered(1, f)
        for r in range(3 * f, 3 * f + 3):
            g[1, r * NX : (r + 1) * NX, :] += dot(xa[f], theirs(1, r))

    twin = 1 - core
    cx16 = cxt[rows(chip, 16), :]
    for part in range(4):
        parts = []
        for j in range(part * 8, part * 8 + 8, 2):
            weights = [[jnp.broadcast_to(rtb[jj, r : r + 1, :], (8, NY)) for r in range(6)] for jj in (j, j + 1)]
            tiles = [[], []]
            for x in range(8):
                src = [g[1, r * NX + x * 8 : r * NX + x * 8 + 8, :] for r in range(6)]
                for n in range(2):
                    total = weights[n][0] * src[0]
                    for r in range(1, 6):
                        total = total + weights[n][r] * src[r]
                    at_x = slice(x * 8, x * 8 + 8)
                    tiles[n].append(e1[j + n, at_x, :] + ge[j + n, at_x, :] * total)
            parts += [jnp.concatenate(t, axis=0) for t in tiles]
        x = dot(cx16, jnp.concatenate(parts, axis=1))
        for c in range(2):
            for j in range(8):
                yo[c, part * 8 + j] = x[c * 8 : c * 8 + 8, j * NY : (j + 1) * NY]
        p8 = rows(part, 8)
        send(yo.at[twin, p8], yr.at[p8], y_s.at[part], y_r.at[part], dom, chip * 2 + twin)

    def step_two(i, _):
        nxt[rows(i), :] = base2[rows(i), :] + forced(1, i)
        return 0

    lax.fori_loop(0, 8, step_two, 0)
    out[core] = yo[core]
    for part in range(4):
        p8 = rows(part, 8)
        arrived(yr.at[p8], y_s.at[part], y_r.at[part])
        out[twin, p8] = yr[p8]

    for c in started:
        c.wait_send()


def finish(nxt_, cur_, y, ztt, cy, nxt, cur, prs, p, sems):
    copies = [pltpu.make_async_copy(nxt_, nxt, sems.at[0]), pltpu.make_async_copy(cur_, cur, sems.at[1])]
    for c in copies:
        c.start()
    for h in range(2):
        a = dot(ztt[...], jnp.concatenate([y[:, :, i].reshape(ZC, NY) for i in range(h * 4, h * 4 + 4)], axis=1))
        a = jnp.concatenate([a[:, n * NY : (n + 1) * NY] for n in range(4)], axis=0)
        p[h * 4 * ZC : (h + 1) * 4 * ZC, :] = dot(a, cy[...])
        c = pltpu.make_async_copy(p.at[rows(h, 4 * ZC)], prs.at[rows(h, 4 * ZC)], sems.at[2 + h])
        c.start()
        copies.append(c)
    for c in copies:
        c.wait()


def table(n):
    k, x = np.arange(n)[:, None], np.arange(n)[None, :]
    return (np.where(k == 0, math.sqrt(1 / n), math.sqrt(2 / n)) * np.cos(math.pi * k * (x + 0.5) / n)).astype(np.float32)


def on_device(modes_now, modes_prev, z_extent, lower_nbr, upper_nbr, x_shift, y_shift):
    slab = modes_now.shape[0]
    flat = jax.ShapeDtypeStruct((slab * ZC, NY), F32)
    cx, cy = table(NX), jnp.asarray(table(NY))
    hbm, vmem = pl.BlockSpec(memory_space=pltpu.HBM), pl.BlockSpec(memory_space=pltpu.VMEM)
    v = lambda *s: pltpu.VMEM(s, F32)
    sm = lambda *s: pltpu.SMEM(s, jnp.int32)
    dma = pltpu.SemaphoreType.DMA
    nxt, cur, y, ztt = pl.pallas_call(
        kernel,
        out_shape=(flat, flat, jax.ShapeDtypeStruct((2, KH, 8, NY), F32), jax.ShapeDtypeStruct((ZC, ZC), F32)),
        in_specs=[pl.BlockSpec(memory_space=pltpu.SMEM)] * 3 + [hbm] * 7,
        out_specs=(vmem,) * 4,
        scratch_shapes=[
            sm(1, 2), sm(1, 2), v(512, NY), v(512, NY), v(NX, NX), v(NX, NX), v(NY, NY),
            v(ZC, 8), v(8, ZC), v(24, ZC), v(KH, 8, NY), v(512, NY), v(512, NY), v(512, NY), v(512, NY), v(512, NY),
            v(64, NY), v(192, NY), v(21, 8, NY), v(6, 8, NY),
            v(2, 6, 8, NY), v(4, 2, 8, NY), v(2, 2, 16, 3, 8, NY), v(2, 2, 4, 3, 8, NY), v(2, 2, 4, 3, 8, NY),
            v(2, 2, 8, 3, 8, NY), v(2, 8, 6, 8, NY), v(2, NX, NX), v(2, NX, NX), v(2, 2, NY, NY), v(6, 8, NY),
            v(2, 8 * NX, NY),
            v(ZC, 8, NY), v(8, KH, 8, NY), v(KH, NX, NY), v(KH, NX, NY), v(2, KH, 8, NY), v(KH, 8, NY),
            dma((7,)), dma((4,)), dma((4,)), dma((2, 2, 16)), dma((2, 2, 16)), dma((2, 2, 4)), dma((2, 2, 4)),
            dma((2, 2, 8)), dma((2, 2, 8)), dma((2, 8)), dma((2, 8)), dma((2, 8)), dma((2, 8)), dma((4,)), dma((4,)),
        ],
        compiler_params=pltpu.CompilerParams(collective_id=0, has_side_effects=True, vmem_limit_bytes=20 * 2**20),
    )(z_extent, lower_nbr, upper_nbr, *[
        pltpu.with_memory_space_constraint(a, pltpu.HBM)
        for a in (
            x_shift, y_shift,
            modes_now.reshape(slab * ZC, NY), modes_prev.reshape(slab * ZC, NY),
            jnp.asarray(cx), jnp.asarray(cx.T.copy()), cy,
        )
    ])
    anyw = pl.BlockSpec(memory_space=pl.ANY)
    outs = pl.pallas_call(
        finish,
        out_shape=(flat,) * 3,
        in_specs=[anyw, anyw, vmem, vmem, vmem],
        out_specs=(hbm,) * 3,
        scratch_shapes=[v(512, NY), dma((4,))],
        compiler_params=pltpu.CompilerParams(vmem_limit_bytes=8 * 2**20),
    )(nxt, cur, y, ztt, cy)
    return tuple(o.reshape(slab, ZC, NY) for o in outs)


def solution(mesh):
    placed = (
        P("split", "dom", None),
        P("split", "dom", None),
        P("dom"),
        P("dom"),
        P("dom"),
        P("dom", None),
        P("dom", None),
    )
    return jax.shard_map(
        on_device,
        mesh=mesh,
        in_specs=placed,
        out_specs=(P("split", "dom", None),) * 3,
        check_vma=False,
    )
```

```python
import math

import jax
import jax.numpy as jnp
import numpy as np
from jax import lax
from jax.experimental import pallas as pl
from jax.experimental.pallas import tpu as pltpu
from jax.sharding import PartitionSpec as P

F32 = jnp.float32
HIGH = lax.Precision.HIGH
XN, ZN, SN = 4, 16, 8
NX, NY, ZC = 64, 128, 64
QUARTER = 0.25
ST1, ST2, ST3 = 270.0 / 180.0, -27.0 / 180.0, 2.0 / 180.0
GAIN = [2.0 * (-1.0) ** n / math.factorial(2 * n + 2) for n in range(12)]
HALF_PI_2 = (math.pi / 2) ** 2
PAIRS = [(a, b) for a in range(6) for b in range(a, 6)]
MESH = pl.DeviceIdType.MESH


def dot(a, b):
    return jnp.dot(a, b, precision=HIGH, preferred_element_type=F32)


def dot_nt(a, b):
    return lax.dot_general(a, b, (((1,), (1,)), ((), ())), precision=HIGH, preferred_element_type=F32)


def gain_of(u):
    g = jnp.full(u.shape, GAIN[-1], F32)
    for c in GAIN[-2::-1]:
        g = g * u + c
    return g


def cos_table(k, x, length):
    n = k * (2.0 * x + 1.0)
    period = 4.0 * length
    rest = n - period * jnp.floor(n / period + 0.5)
    w = (math.pi / 2) * (rest / length)
    u = w * w
    scale = jnp.where(k == 0, jnp.sqrt(1.0 / length), jnp.sqrt(2.0 / length))
    return scale * (1.0 - 0.5 * u * gain_of(u))


def iota(shape, dim):
    return lax.broadcasted_iota(jnp.int32, shape, dim).astype(F32)


def low_rows(q1, q2, q3):
    return [ST1 * q1 + ST2 * q2 + ST3 * q3, ST2 * q1 + ST3 * q2, ST3 * q1]


def rows(i, n=ZC):
    return pl.ds(pl.multiple_of(i * n, n), n)


WINDOWS = [
    sorted([(i, d) for i in range(XN) for d in ds], key=lambda p: min(p[0], XN - p[0]) + abs(p[1]))
    for ds in (range(-1, 3), range(-2, 2))
]
GREET = [(i, d) for d in (-2, 2, -1, 1, 0) for i in (2, 1, 3, 0) if (i, d) != (0, 0)]


def kernel(
    ext, low, upp, xs_, ys_, m0_, m1_, cx_, cxt_, cy_,
    nxt, cur, out, ztt,
    xs, ys, m0, m1, cx, cxt, cy,
    rt, rtt, w2, rtb, mz, b1, gn, h0, base2, sscr, kscr, kt, sb, st, nb, near, sel, far, aa, bb, xa, xb, yab, gb, g,
    hs, hb, ge, e0, yo, yr,
    in_s, nb_s, nb_r, near_s, near_r, far_s, far_r, aa_s, aa_r, bb_s, bb_r, h_s, h_r, y_s, y_r,
):
    dom, me = lax.axis_index("dom"), lax.axis_index("split")
    px, pz = dom // ZN, lax.rem(dom, ZN)

    loads = [
        pltpu.make_async_copy(a, b, in_s.at[n])
        for n, (a, b) in enumerate([(m0_, m0), (xs_, xs), (ys_, ys), (cx_, cx), (cy_, cy), (m1_, m1), (cxt_, cxt)])
    ]
    for c in loads:
        c.start()

    def at(dx, dz):
        return lax.rem(px + dx + XN, XN) * ZN + lax.rem(pz + dz + ZN, ZN)

    def other(t):
        return lax.rem(me + t, SN)

    barrier = pltpu.get_barrier_semaphore()

    def greet(d, s):
        pl.semaphore_signal(barrier, inc=1, device_id=(d, s), device_id_type=MESH)

    for k in (2, 1, 3):
        greet(at(0, 4 * k), me)
    for i, d in GREET:
        greet(at(i, d), me)
    for t in range(1, SN):
        greet(dom, other(t))

    started = []

    def drained():
        while started:
            started.pop(0).wait_send()


    def send(src, dst, ss, rs, d, s):
        c = pltpu.make_async_remote_copy(
            src_ref=src, dst_ref=dst, send_sem=ss, recv_sem=rs, device_id=(d, s), device_id_type=MESH
        )
        c.start()
        started.append(c)

    def arrived(dst, ss, rs):
        pltpu.make_async_remote_copy(
            src_ref=dst, dst_ref=dst, send_sem=ss, recv_sem=rs, device_id=(dom, me), device_id_type=MESH
        ).wait_recv()

    length = ext[0].astype(F32)

    def row_of(r):
        return jnp.where(r < 3, r, r + (length - 6.0))

    def row_table(k, r):
        return jnp.where((k < length) & (r < 6), cos_table(k, row_of(r), jnp.full(k.shape, length)), 0.0)

    rtt[...] = row_table(iota((8, ZC), 1), iota((8, ZC), 0))
    lowf, uppf = low[0].astype(F32), upp[0].astype(F32)
    nb[0, 0] = jnp.full((8, 128), lowf)
    nb[0, 1] = jnp.full((8, 128), uppf)
    loads[0].wait()
    for i in range(8):
        sscr[i * 8 : i * 8 + 8, :] = dot(rtt[...], m0[i * ZC : (i + 1) * ZC, :])
    for r in range(6):
        st[0, r] = sscr[pl.ds(r, 8, stride=8), :]
    pl.semaphore_wait(barrier, len(GREET) + 3 + SN - 1)

    def strip_rows(f):
        return slice(3, 6) if f == 0 else slice(0, 3)

    def send_near(step):
        for f in range(2):
            for n in range(15, 0, -1):
                i, d = WINDOWS[f][n]
                send(
                    st.at[step, strip_rows(f)], near.at[step, f, n],
                    near_s.at[step, f, n], near_r.at[step, f, n], at(i, d), me,
                )

    for k in (2, 1, 3):
        send(nb.at[0], nb.at[k], nb_s.at[k], nb_r.at[k], at(0, -4 * k), me)
    send_near(0)

    for c in loads[1:5]:
        c.wait()

    for f in range(2):
        for c, n, move, is_x in ((cy, NY, ys[0, f], False), (cx, NX, xs[0, f], True)):
            move = move.astype(F32)
            row, col = iota((n, n), 0), iota((n, n), 1)
            put = (col == row + move).astype(F32)
            tab = c[...]
            seen = ((col + move >= 0) & (col + move < n)).astype(F32)
            moved = dot(tab, put)
            b = dot_nt(tab * seen, tab)
            if is_x:
                has = jnp.where(jnp.full((n, n), uppf if f else lowf) >= 0, QUARTER, 0.0)
                xa[f] = dot_nt(moved, tab) * has
                xb[f] = -b * has
            else:
                yab[f, 0] = dot_nt(tab, moved)
                yab[f, 1] = b

    def own_part(step):
        p = [st[step, r] for r in range(6)]
        for f, part in enumerate((low_rows(p[0], p[1], p[2]), low_rows(p[5], p[4], p[3])[::-1])):
            bb[step, me, 3 * f : 3 * f + 3] = dot(jnp.concatenate(part, axis=0), yab[f, 1]).reshape(3, 8, NY)
        for t in range(1, SN):
            send(bb.at[step, me], bb.at[step, me], bb_s.at[step, t], bb_r.at[step, t], dom, other(t))

    def to_far(step, f):
        acc = [[jnp.zeros((8, NY), F32)] * 3 for _ in range(4)]
        rows_f = strip_rows(f)
        for n, (i, d) in enumerate(WINDOWS[f]):
            if n == 0:
                block = [st[step, r] for r in range(rows_f.start, rows_f.stop)]
            else:
                arrived(near.at[step, f, n], near_s.at[step, f, n], near_r.at[step, f, n])
                block = [near[step, f, n, r] for r in range(3)]
            who = at(-i, -d).astype(F32)
            for k in range(4):
                hit = nb[k, f] == who
                acc[k] = [jnp.where(hit, v, a) for v, a in zip(block, acc[k])]
        for k in (2, 1, 3, 0):
            for r in range(3):
                sel[step, f, k, r] = acc[k][r]
            if k:
                send(
                    sel.at[step, f, k], far.at[step, f, k],
                    far_s.at[step, f, k], far_r.at[step, f, k], at(0, 4 * k), me,
                )

    def from_far(step, f):
        q = [sel[step, f, 0, r] for r in range(3)]
        for k in (1, 3, 2):
            arrived(far.at[step, f, k], far_s.at[step, f, k], far_r.at[step, f, k])
            q = [a + far[step, f, k, r] for r, a in enumerate(q)]
        part = low_rows(*q)[::-1] if f else low_rows(*q[::-1])
        aa[step, f, me] = dot(jnp.concatenate(part, axis=0), yab[f, 0]).reshape(3, 8, NY)
        for t in range(1, SN):
            send(aa.at[step, f, me], aa.at[step, f, me], aa_s.at[step, f, t], aa_r.at[step, f, t], dom, other(t))

    def gathered_own(step):
        for t in range(1, SN):
            arrived(bb.at[step, other(SN - t)], bb_s.at[step, t], bb_r.at[step, t])

    def gathered(step, f):
        for t in range(1, SN):
            arrived(aa.at[step, f, other(SN - t)], aa_s.at[step, f, t], aa_r.at[step, f, t])

    def theirs(step, r):
        return aa[step, r // 3, :, r % 3].reshape(NX, NY)

    def ours(step, r):
        return bb[step, :, r].reshape(NX, NY)

    def forced(step, i):
        return gn[rows(i), :] * dot(rt[...], g[step, pl.ds(me * 8 + i, 8, stride=NX), :])

    own_part(0)

    kz = iota((ZC, NY), 0)
    live = kz < length
    lv = jnp.full((ZC, NY), length)
    flat = kz / lv
    flat = flat * flat + (iota((ZC, NY), 1) / NY) ** 2

    def twice(i):
        kx = (me * 8 + i).astype(F32) / NX
        return HALF_PI_2 * (flat + kx * kx)

    loads[5].wait()

    def bases(i, _):
        u = twice(i)
        gain = gain_of(u)
        tw = 2.0 - u * gain
        m = jnp.where(live, m0[rows(i), :], 0.0)
        base = tw * m - jnp.where(live, m1[rows(i), :], 0.0)
        mz[rows(i), :] = m
        gn[rows(i), :] = gain
        b1[rows(i), :] = base
        h0[rows(i), :] = tw * base - m
        return 0

    lax.fori_loop(0, 8, bases, 0)
    for k in (1, 3, 2):
        arrived(nb.at[k], nb_s.at[k], nb_r.at[k])
    to_far(0, 0)
    to_far(0, 1)

    def turn(k, _):
        hs[k] = h0[pl.ds(k, 8, stride=ZC), :]
        return 0

    lax.fori_loop(0, ZC, turn, 0, unroll=8)

    for t in range(1, SN):
        send(hs.at[rows(other(t), 8)], hb.at[me], h_s.at[t], h_r.at[t], dom, other(t))
    hb[me] = hs[rows(me, 8)]
    for n, (a, b) in enumerate(PAIRS):
        w2[n : n + 1, :] = rtt[a : a + 1, :] * rtt[b : b + 1, :]
    w2[21:24, :] = jnp.zeros((3, ZC), F32)

    def strips(i, _):
        sscr[rows(i, 8), :] = dot(rtt[...], b1[rows(i), :])
        kscr[rows(i, 24), :] = dot(w2[...], gn[rows(i), :])
        return 0

    lax.fori_loop(0, 8, strips, 0)
    for r in range(6):
        sb[r] = sscr[pl.ds(r, 8, stride=8), :]
    for n in range(21):
        kt[n] = kscr[pl.ds(n, 8, stride=24), :]
    kx2 = (iota((NX, NY), 0) / NX) ** 2 + (iota((NX, NY), 1) / NY) ** 2

    def angles(k):
        z = jnp.full((NX, NY), k.astype(F32)) / lv
        return HALF_PI_2 * (kx2 + z * z)

    def gains(k, _):
        ge[k] = gain_of(angles(k))
        return 0

    lax.fori_loop(0, ZC, gains, 0)
    gathered_own(0)
    for r in range(6):
        gb[r] = dot(xb[r // 3, rows(me, 8), :], ours(0, r))
    from_far(0, 0)
    from_far(0, 1)

    rt[...] = row_table(iota((ZC, 8), 0), iota((ZC, 8), 1))
    kk, zz = iota((ZC, ZC), 1), iota((ZC, ZC), 0)
    ztt[...] = jnp.where((kk < length) & (zz < length), cos_table(kk, zz, jnp.full((ZC, ZC), length)), 0.0)
    g1 = []
    for f in range(2):
        gathered(0, f)
        for r in range(3 * f, 3 * f + 3):
            g1.append(gb[r] + dot(xa[f, rows(me, 8), :], theirs(0, r)))
    for r in range(6):
        s = sb[r]
        for q in range(6):
            s = s + kt[PAIRS.index((min(r, q), max(r, q)))] * g1[q]
        st[1, r] = s
    send_near(1)
    own_part(1)
    for step in range(2):
        g[step, 6 * NX :, :] = jnp.zeros((2 * NX, NY), F32)
    for r in range(6):
        g[0, r * NX : (r + 1) * NX, :] = dot(xb[r // 3], ours(0, r)) + dot(xa[r // 3], theirs(0, r))
    shape = (ZC, 8, NY)
    rtb[...] = row_table(iota(shape, 0), iota(shape, 1))
    for t in range(1, SN):
        arrived(hb.at[other(SN - t)], h_s.at[t], h_r.at[t])
    loads[6].wait()

    def early(j, _):
        k = me * 8 + j
        gain = ge[k]
        total = rtb[k, 0:1, :] * g[0, 0:NX, :]
        for r in range(1, 6):
            total = total + rtb[k, r : r + 1, :] * g[0, r * NX : (r + 1) * NX, :]
        e = hb[:, j].reshape(NX, NY) + gain * (2.0 - angles(k) * gain) * total
        yo[:, j] = dot(cxt[...], e).reshape(SN, 8, NY)
        return 0

    lax.fori_loop(0, 8, early, 0)
    to_far(1, 0)
    to_far(1, 1)

    def step_one(i, _):
        m = b1[rows(i), :] + forced(0, i)
        cur[rows(i), :] = m
        base2[rows(i), :] = (2.0 - twice(i) * gn[rows(i), :]) * m - mz[rows(i), :]
        return 0

    drained()
    for t in range(1, SN):
        send(yo.at[other(t)], yr.at[rows(me, 8)], y_s.at[t], y_r.at[t], dom, other(t))
    yr[rows(me, 8)] = yo[me]
    gathered_own(1)
    for r in range(6):
        g[1, r * NX : (r + 1) * NX, :] = dot(xb[r // 3], ours(1, r))
    lax.fori_loop(0, 8, step_one, 0)
    for t in range(1, SN):
        arrived(yr.at[rows(other(SN - t), 8)], y_s.at[t], y_r.at[t])
    from_far(1, 0)
    from_far(1, 1)
    drained()

    def face(f):
        gathered(1, f)
        for r in range(3 * f, 3 * f + 3):
            g[1, r * NX : (r + 1) * NX, :] += dot(xa[f], theirs(1, r))

    def weights(k, f):
        return [jnp.broadcast_to(rtb[k, 3 * f + r : 3 * f + r + 1, :], (8, NY)) for r in range(3)]

    def sources(f, x):
        return [g[1, r * NX + x * 8 : r * NX + x * 8 + 8, :] for r in range(3 * f, 3 * f + 3)]

    face(0)

    def lower_part(i, _):
        ws = [weights(i * 4 + n, 0) for n in range(4)]
        for x in range(8):
            src = sources(0, x)
            for n, w in enumerate(ws):
                e0[i * 4 + n, x * 8 : x * 8 + 8, :] = w[0] * src[0] + w[1] * src[1] + w[2] * src[2]
        return 0

    lax.fori_loop(0, ZC // 4, lower_part, 0)
    face(1)
    cx8 = cxt[rows(me, 8), :]
    for i in range(8):
        nxt[i * ZC : (i + 1) * ZC, :] = base2[i * ZC : (i + 1) * ZC, :] + forced(1, i)

    def late(i, _):
        parts = []
        for j in range(0, 8, 4):
            ws = [weights(i * 8 + j + n, 1) for n in range(4)]
            tiles = [[] for _ in ws]
            for x in range(8):
                src = sources(1, x)
                at_x = slice(x * 8, x * 8 + 8)
                for n, w in enumerate(ws):
                    k = i * 8 + j + n
                    total = e0[k, at_x, :] + w[0] * src[0] + w[1] * src[1] + w[2] * src[2]
                    tiles[n].append(ge[k, at_x, :] * total)
            parts += [jnp.concatenate(t, axis=0) for t in tiles]
        x = dot(cx8, jnp.concatenate(parts, axis=1))
        for j in range(8):
            out[i * 8 + j] = yr[i * 8 + j] + x[:, j * NY : (j + 1) * NY]
        return 0

    for i in range(8):
        late(i, 0)
    drained()


def finish(nxt_, cur_, y, ztt, cy, nxt, cur, prs, p, sems):
    copies = [pltpu.make_async_copy(nxt_, nxt, sems.at[0]), pltpu.make_async_copy(cur_, cur, sems.at[1])]
    for c in copies:
        c.start()
    for h in range(2):
        a = dot(ztt[...], jnp.concatenate([y[:, i, :] for i in range(h * 4, h * 4 + 4)], axis=1))
        a = jnp.concatenate([a[:, n * NY : (n + 1) * NY] for n in range(4)], axis=0)
        p[h * 4 * ZC : (h + 1) * 4 * ZC, :] = dot(a, cy[...])
        c = pltpu.make_async_copy(p.at[rows(h, 4 * ZC)], prs.at[rows(h, 4 * ZC)], sems.at[2 + h])
        c.start()
        copies.append(c)
    for c in copies:
        c.wait()


def table(n):
    k, x = np.arange(n)[:, None], np.arange(n)[None, :]
    return (np.where(k == 0, math.sqrt(1 / n), math.sqrt(2 / n)) * np.cos(math.pi * k * (x + 0.5) / n)).astype(np.float32)


def on_device(modes_now, modes_prev, z_extent, lower_nbr, upper_nbr, x_shift, y_shift):
    slab = modes_now.shape[0]
    flat = jax.ShapeDtypeStruct((slab * ZC, NY), F32)
    cx, cy = table(NX), jnp.asarray(table(NY))
    hbm, vmem = pl.BlockSpec(memory_space=pltpu.HBM), pl.BlockSpec(memory_space=pltpu.VMEM)
    v = lambda *s: pltpu.VMEM(s, F32)
    sm = lambda *s: pltpu.SMEM(s, jnp.int32)
    dma = pltpu.SemaphoreType.DMA
    nxt, cur, y, ztt = pl.pallas_call(
        kernel,
        out_shape=(flat, flat, jax.ShapeDtypeStruct((ZC, 8, NY), F32), jax.ShapeDtypeStruct((ZC, ZC), F32)),
        in_specs=[pl.BlockSpec(memory_space=pltpu.SMEM)] * 3 + [hbm] * 7,
        out_specs=(vmem,) * 4,
        scratch_shapes=[
            sm(1, 2), sm(1, 2), v(512, NY), v(512, NY), v(NX, NX), v(NX, NX), v(NY, NY),
            v(ZC, 8), v(8, ZC), v(24, ZC), v(ZC, 8, NY), v(512, NY), v(512, NY), v(512, NY), v(512, NY), v(512, NY),
            v(64, NY), v(192, NY), v(21, 8, NY), v(6, 8, NY),
            v(2, 6, 8, NY), v(4, 2, 8, NY), v(2, 2, 16, 3, 8, NY), v(2, 2, 4, 3, 8, NY), v(2, 2, 4, 3, 8, NY),
            v(2, 2, 8, 3, 8, NY), v(2, 8, 6, 8, NY), v(2, NX, NX), v(2, NX, NX), v(2, 2, NY, NY), v(6, 8, NY),
            v(2, 8 * NX, NY),
            v(ZC, 8, NY), v(8, 8, 8, NY), v(ZC, NX, NY), v(ZC, NX, NY), v(8, 8, 8, NY), v(ZC, 8, NY),
            dma((7,)), dma((4,)), dma((4,)), dma((2, 2, 16)), dma((2, 2, 16)), dma((2, 2, 4)), dma((2, 2, 4)),
            dma((2, 2, 8)), dma((2, 2, 8)), dma((2, 8)), dma((2, 8)), dma((8,)), dma((8,)), dma((8,)), dma((8,)),
        ],
        compiler_params=pltpu.CompilerParams(collective_id=0, has_side_effects=True, vmem_limit_bytes=20 * 2**20),
    )(z_extent, lower_nbr, upper_nbr, *[
        pltpu.with_memory_space_constraint(a, pltpu.HBM)
        for a in (
            x_shift, y_shift,
            modes_now.reshape(slab * ZC, NY), modes_prev.reshape(slab * ZC, NY),
            jnp.asarray(cx), jnp.asarray(cx.T.copy()), cy,
        )
    ])
    anyw = pl.BlockSpec(memory_space=pl.ANY)
    outs = pl.pallas_call(
        finish,
        out_shape=(flat,) * 3,
        in_specs=[anyw, anyw, vmem, vmem, vmem],
        out_specs=(hbm,) * 3,
        scratch_shapes=[v(512, NY), dma((4,))],
        compiler_params=pltpu.CompilerParams(vmem_limit_bytes=8 * 2**20),
    )(nxt, cur, y, ztt, cy)
    return tuple(o.reshape(slab, ZC, NY) for o in outs)


def solution(mesh):
    placed = (
        P("split", "dom", None),
        P("split", "dom", None),
        P("dom"),
        P("dom"),
        P("dom"),
        P("dom", None),
        P("dom", None),
    )
    return jax.shard_map(
        on_device,
        mesh=mesh,
        in_specs=placed,
        out_specs=(P("split", "dom", None),) * 3,
        check_vma=False,
    )
```

```python
import math

import jax
import jax.numpy as jnp
import numpy as np
from jax import lax
from jax.experimental import pallas as pl
from jax.experimental.pallas import tpu as pltpu
from jax.sharding import PartitionSpec as P

F32 = jnp.float32
HIGH = lax.Precision.HIGH
XN, ZN, SN = 4, 16, 8
NX, NY, ZC = 64, 128, 64
QUARTER = 0.25
ST1, ST2, ST3 = 270.0 / 180.0, -27.0 / 180.0, 2.0 / 180.0
GAIN = [2.0 * (-1.0) ** n / math.factorial(2 * n + 2) for n in range(12)]
HALF_PI_2 = (math.pi / 2) ** 2
PAIRS = [(a, b) for a in range(6) for b in range(a, 6)]
MESH = pl.DeviceIdType.MESH


def dot(a, b):
    return jnp.dot(a, b, precision=HIGH, preferred_element_type=F32)


def dot_nt(a, b):
    return lax.dot_general(a, b, (((1,), (1,)), ((), ())), precision=HIGH, preferred_element_type=F32)


def gain_of(u):
    g = jnp.full(u.shape, GAIN[-1], F32)
    for c in GAIN[-2::-1]:
        g = g * u + c
    return g


def cos_table(k, x, length):
    n = k * (2.0 * x + 1.0)
    period = 4.0 * length
    rest = n - period * jnp.floor(n / period + 0.5)
    w = (math.pi / 2) * (rest / length)
    u = w * w
    scale = jnp.where(k == 0, jnp.sqrt(1.0 / length), jnp.sqrt(2.0 / length))
    return scale * (1.0 - 0.5 * u * gain_of(u))


def iota(shape, dim):
    return lax.broadcasted_iota(jnp.int32, shape, dim).astype(F32)


def low_rows(q1, q2, q3):
    return [ST1 * q1 + ST2 * q2 + ST3 * q3, ST2 * q1 + ST3 * q2, ST3 * q1]


def rows(i, n=ZC):
    return pl.ds(pl.multiple_of(i * n, n), n)


WINDOWS = [
    sorted([(i, d) for i in range(XN) for d in ds], key=lambda p: min(p[0], XN - p[0]) + abs(p[1]))
    for ds in (range(-1, 3), range(-2, 2))
]
GREET = [(i, d) for d in (-2, 2, -1, 1, 0) for i in (2, 1, 3, 0) if (i, d) != (0, 0)]


def kernel(
    ext, low, upp, xs_, ys_, m0_, m1_, cx_, cxt_, cy_,
    nxt, cur, out, ztt,
    xs, ys, m0, m1, cx, cxt, cy,
    rt, rtt, w2, rtb, mz, b1, gn, h0, base2, sscr, kscr, kt, sb, st, nb, near, sel, far, aa, bb, xa, xb, yab, gb, g,
    hs, hb, ge, e0, yo, yr,
    in_s, nb_s, nb_r, near_s, near_r, far_s, far_r, aa_s, aa_r, bb_s, bb_r, h_s, h_r, y_s, y_r,
):
    dom, me = lax.axis_index("dom"), lax.axis_index("split")
    px, pz = dom // ZN, lax.rem(dom, ZN)

    loads = [
        pltpu.make_async_copy(a, b, in_s.at[n])
        for n, (a, b) in enumerate([(m0_, m0), (xs_, xs), (ys_, ys), (cx_, cx), (cy_, cy), (m1_, m1), (cxt_, cxt)])
    ]
    for c in loads:
        c.start()

    def at(dx, dz):
        return lax.rem(px + dx + XN, XN) * ZN + lax.rem(pz + dz + ZN, ZN)

    def other(t):
        return lax.rem(me + t, SN)

    barrier = pltpu.get_barrier_semaphore()

    def greet(d, s):
        pl.semaphore_signal(barrier, inc=1, device_id=(d, s), device_id_type=MESH)

    for k in (2, 1, 3):
        greet(at(0, 4 * k), me)
    for i, d in GREET:
        greet(at(i, d), me)
    for t in range(1, SN):
        greet(dom, other(t))

    started = []

    def send(src, dst, ss, rs, d, s):
        pltpu.make_async_remote_copy(
            src_ref=src, dst_ref=dst, send_sem=ss, recv_sem=rs, device_id=(d, s), device_id_type=MESH
        ).start()

    def group(whole, ss, rs):
        return pltpu.make_async_remote_copy(
            src_ref=whole, dst_ref=whole, send_sem=ss, recv_sem=rs, device_id=(dom, me), device_id_type=MESH
        )

    def near_group(step, f):
        return group(near.at[step, f, 1:16], near_s.at[step, f], near_r.at[step, f])

    def far_group(step, f):
        return group(far.at[step, f, 1:4], far_s.at[step, f], far_r.at[step, f])

    def aa_group(step, f):
        return group(aa.at[step, f, 0:7], aa_s.at[step, f], aa_r.at[step, f])

    def bb_group(step):
        return group(bb.at[step, 0:7], bb_s.at[step], bb_r.at[step])

    nb_group, h_group, y_group = group(nb.at[1:4], nb_s, nb_r), group(hb.at[0:7], h_s, h_r), group(yr.at[0:56], y_s, y_r)

    def drained():
        while started:
            started.pop(0).wait_send()

    length = ext[0].astype(F32)

    def row_of(r):
        return jnp.where(r < 3, r, r + (length - 6.0))

    def row_table(k, r):
        return jnp.where((k < length) & (r < 6), cos_table(k, row_of(r), jnp.full(k.shape, length)), 0.0)

    rtt[...] = row_table(iota((8, ZC), 1), iota((8, ZC), 0))
    lowf, uppf = low[0].astype(F32), upp[0].astype(F32)
    nb[0, 0] = jnp.full((8, 128), lowf)
    nb[0, 1] = jnp.full((8, 128), uppf)
    loads[0].wait()
    for i in range(8):
        sscr[i * 8 : i * 8 + 8, :] = dot(rtt[...], m0[i * ZC : (i + 1) * ZC, :])
    for r in range(6):
        st[0, r] = sscr[pl.ds(r, 8, stride=8), :]
    pl.semaphore_wait(barrier, len(GREET) + 3 + SN - 1)

    def strip_rows(f):
        return slice(3, 6) if f == 0 else slice(0, 3)

    def send_near(step):
        for f in range(2):
            for n in range(15, 0, -1):
                i, d = WINDOWS[f][n]
                send(st.at[step, strip_rows(f)], near.at[step, f, n], near_s.at[step, f], near_r.at[step, f], at(i, d), me)
            started.append(near_group(step, f))

    for k in (2, 1, 3):
        send(nb.at[0], nb.at[k], nb_s, nb_r, at(0, -4 * k), me)
    started.append(nb_group)
    send_near(0)

    for c in loads[1:5]:
        c.wait()

    for f in range(2):
        for c, n, move, is_x in ((cy, NY, ys[0, f], False), (cx, NX, xs[0, f], True)):
            move = move.astype(F32)
            row, col = iota((n, n), 0), iota((n, n), 1)
            put = (col == row + move).astype(F32)
            tab = c[...]
            seen = ((col + move >= 0) & (col + move < n)).astype(F32)
            moved = dot(tab, put)
            b = dot_nt(tab * seen, tab)
            if is_x:
                has = jnp.where(jnp.full((n, n), uppf if f else lowf) >= 0, QUARTER, 0.0)
                xa[f] = dot_nt(moved, tab) * has
                xb[f] = -b * has
            else:
                yab[f, 0] = dot_nt(tab, moved)
                yab[f, 1] = b

    def own_part(step):
        p = [st[step, r] for r in range(6)]
        for f, part in enumerate((low_rows(p[0], p[1], p[2]), low_rows(p[5], p[4], p[3])[::-1])):
            bb[step, me, 3 * f : 3 * f + 3] = dot(jnp.concatenate(part, axis=0), yab[f, 1]).reshape(3, 8, NY)
        for t in range(1, SN):
            send(bb.at[step, me], bb.at[step, me], bb_s.at[step], bb_r.at[step], dom, other(t))
        started.append(bb_group(step))

    def to_far(step, f):
        acc = [[jnp.zeros((8, NY), F32)] * 3 for _ in range(4)]
        rows_f = strip_rows(f)
        near_group(step, f).wait_recv()
        for n, (i, d) in enumerate(WINDOWS[f]):
            if n == 0:
                block = [st[step, r] for r in range(rows_f.start, rows_f.stop)]
            else:
                block = [near[step, f, n, r] for r in range(3)]
            who = at(-i, -d).astype(F32)
            for k in range(4):
                hit = nb[k, f] == who
                acc[k] = [jnp.where(hit, v, a) for v, a in zip(block, acc[k])]
        for k in (2, 1, 3, 0):
            for r in range(3):
                sel[step, f, k, r] = acc[k][r]
            if k:
                send(sel.at[step, f, k], far.at[step, f, k], far_s.at[step, f], far_r.at[step, f], at(0, 4 * k), me)
        started.append(far_group(step, f))

    def from_far(step, f):
        q = [sel[step, f, 0, r] for r in range(3)]
        far_group(step, f).wait_recv()
        for k in (1, 3, 2):
            q = [a + far[step, f, k, r] for r, a in enumerate(q)]
        part = low_rows(*q)[::-1] if f else low_rows(*q[::-1])
        aa[step, f, me] = dot(jnp.concatenate(part, axis=0), yab[f, 0]).reshape(3, 8, NY)
        for t in range(1, SN):
            send(aa.at[step, f, me], aa.at[step, f, me], aa_s.at[step, f], aa_r.at[step, f], dom, other(t))
        started.append(aa_group(step, f))

    def theirs(step, r):
        return aa[step, r // 3, :, r % 3].reshape(NX, NY)

    def ours(step, r):
        return bb[step, :, r].reshape(NX, NY)

    def forced(step, i):
        return gn[rows(i), :] * dot(rt[...], g[step, pl.ds(me * 8 + i, 8, stride=NX), :])

    own_part(0)

    kz = iota((ZC, NY), 0)
    live = kz < length
    lv = jnp.full((ZC, NY), length)
    flat = kz / lv
    flat = flat * flat + (iota((ZC, NY), 1) / NY) ** 2

    def twice(i):
        kx = (me * 8 + i).astype(F32) / NX
        return HALF_PI_2 * (flat + kx * kx)

    loads[5].wait()

    def bases(i, _):
        u = twice(i)
        gain = gain_of(u)
        tw = 2.0 - u * gain
        m = jnp.where(live, m0[rows(i), :], 0.0)
        base = tw * m - jnp.where(live, m1[rows(i), :], 0.0)
        mz[rows(i), :] = m
        gn[rows(i), :] = gain
        b1[rows(i), :] = base
        h0[rows(i), :] = tw * base - m
        return 0

    lax.fori_loop(0, 8, bases, 0)
    nb_group.wait_recv()
    to_far(0, 0)
    to_far(0, 1)

    def turn(k, _):
        hs[k] = h0[pl.ds(k, 8, stride=ZC), :]
        return 0

    lax.fori_loop(0, ZC, turn, 0, unroll=8)

    for t in range(1, SN):
        send(hs.at[rows(other(t), 8)], hb.at[me], h_s, h_r, dom, other(t))
    started.append(h_group)
    hb[me] = hs[rows(me, 8)]
    for n, (a, b) in enumerate(PAIRS):
        w2[n : n + 1, :] = rtt[a : a + 1, :] * rtt[b : b + 1, :]
    w2[21:24, :] = jnp.zeros((3, ZC), F32)

    def strips(i, _):
        sscr[rows(i, 8), :] = dot(rtt[...], b1[rows(i), :])
        kscr[rows(i, 24), :] = dot(w2[...], gn[rows(i), :])
        return 0

    lax.fori_loop(0, 8, strips, 0)
    for r in range(6):
        sb[r] = sscr[pl.ds(r, 8, stride=8), :]
    for n in range(21):
        kt[n] = kscr[pl.ds(n, 8, stride=24), :]
    kx2 = (iota((NX, NY), 0) / NX) ** 2 + (iota((NX, NY), 1) / NY) ** 2

    def angles(k):
        z = jnp.full((NX, NY), k.astype(F32)) / lv
        return HALF_PI_2 * (kx2 + z * z)

    def gains(k, _):
        ge[k] = gain_of(angles(k))
        return 0

    lax.fori_loop(0, ZC, gains, 0)
    bb_group(0).wait_recv()
    for r in range(6):
        gb[r] = dot(xb[r // 3, rows(me, 8), :], ours(0, r))
    from_far(0, 0)
    from_far(0, 1)

    rt[...] = row_table(iota((ZC, 8), 0), iota((ZC, 8), 1))
    kk, zz = iota((ZC, ZC), 1), iota((ZC, ZC), 0)
    ztt[...] = jnp.where((kk < length) & (zz < length), cos_table(kk, zz, jnp.full((ZC, ZC), length)), 0.0)
    g1 = []
    for f in range(2):
        aa_group(0, f).wait_recv()
        for r in range(3 * f, 3 * f + 3):
            g1.append(gb[r] + dot(xa[f, rows(me, 8), :], theirs(0, r)))
    for r in range(6):
        s = sb[r]
        for q in range(6):
            s = s + kt[PAIRS.index((min(r, q), max(r, q)))] * g1[q]
        st[1, r] = s
    send_near(1)
    own_part(1)
    for step in range(2):
        g[step, 6 * NX :, :] = jnp.zeros((2 * NX, NY), F32)
    for r in range(6):
        g[0, r * NX : (r + 1) * NX, :] = dot(xb[r // 3], ours(0, r)) + dot(xa[r // 3], theirs(0, r))
    shape = (ZC, 8, NY)
    rtb[...] = row_table(iota(shape, 0), iota(shape, 1))
    h_group.wait_recv()
    loads[6].wait()

    def early(j, _):
        k = me * 8 + j
        gain = ge[k]
        total = rtb[k, 0:1, :] * g[0, 0:NX, :]
        for r in range(1, 6):
            total = total + rtb[k, r : r + 1, :] * g[0, r * NX : (r + 1) * NX, :]
        e = hb[:, j].reshape(NX, NY) + gain * (2.0 - angles(k) * gain) * total
        yo[:, j] = dot(cxt[...], e).reshape(SN, 8, NY)
        return 0

    lax.fori_loop(0, 8, early, 0)
    to_far(1, 0)
    to_far(1, 1)

    def step_one(i, _):
        m = b1[rows(i), :] + forced(0, i)
        cur[rows(i), :] = m
        base2[rows(i), :] = (2.0 - twice(i) * gn[rows(i), :]) * m - mz[rows(i), :]
        return 0

    drained()
    for t in range(1, SN):
        send(yo.at[other(t)], yr.at[rows(me, 8)], y_s, y_r, dom, other(t))
    started.append(y_group)
    yr[rows(me, 8)] = yo[me]
    bb_group(1).wait_recv()
    for r in range(6):
        g[1, r * NX : (r + 1) * NX, :] = dot(xb[r // 3], ours(1, r))
    lax.fori_loop(0, 8, step_one, 0)
    y_group.wait_recv()
    from_far(1, 0)
    from_far(1, 1)
    drained()

    def face(f):
        aa_group(1, f).wait_recv()
        for r in range(3 * f, 3 * f + 3):
            g[1, r * NX : (r + 1) * NX, :] += dot(xa[f], theirs(1, r))

    def weights(k, f):
        return [jnp.broadcast_to(rtb[k, 3 * f + r : 3 * f + r + 1, :], (8, NY)) for r in range(3)]

    def sources(f, x):
        return [g[1, r * NX + x * 8 : r * NX + x * 8 + 8, :] for r in range(3 * f, 3 * f + 3)]

    face(0)

    def lower_part(i, _):
        ws = [weights(i * 4 + n, 0) for n in range(4)]
        for x in range(8):
            src = sources(0, x)
            for n, w in enumerate(ws):
                e0[i * 4 + n, x * 8 : x * 8 + 8, :] = w[0] * src[0] + w[1] * src[1] + w[2] * src[2]
        return 0

    lax.fori_loop(0, ZC // 4, lower_part, 0)
    face(1)
    cx8 = cxt[rows(me, 8), :]
    for i in range(8):
        nxt[i * ZC : (i + 1) * ZC, :] = base2[i * ZC : (i + 1) * ZC, :] + forced(1, i)

    def late(i, _):
        parts = []
        for j in range(0, 8, 4):
            ws = [weights(i * 8 + j + n, 1) for n in range(4)]
            tiles = [[] for _ in ws]
            for x in range(8):
                src = sources(1, x)
                at_x = slice(x * 8, x * 8 + 8)
                for n, w in enumerate(ws):
                    k = i * 8 + j + n
                    total = e0[k, at_x, :] + w[0] * src[0] + w[1] * src[1] + w[2] * src[2]
                    tiles[n].append(ge[k, at_x, :] * total)
            parts += [jnp.concatenate(t, axis=0) for t in tiles]
        x = dot(cx8, jnp.concatenate(parts, axis=1))
        for j in range(8):
            out[i * 8 + j] = yr[i * 8 + j] + x[:, j * NY : (j + 1) * NY]
        return 0

    for i in range(8):
        late(i, 0)
    drained()


def finish(nxt_, cur_, y, ztt, cy, nxt, cur, prs, p, sems):
    copies = [pltpu.make_async_copy(nxt_, nxt, sems.at[0]), pltpu.make_async_copy(cur_, cur, sems.at[1])]
    for c in copies:
        c.start()
    for h in range(2):
        a = dot(ztt[...], jnp.concatenate([y[:, i, :] for i in range(h * 4, h * 4 + 4)], axis=1))
        a = jnp.concatenate([a[:, n * NY : (n + 1) * NY] for n in range(4)], axis=0)
        p[h * 4 * ZC : (h + 1) * 4 * ZC, :] = dot(a, cy[...])
        c = pltpu.make_async_copy(p.at[rows(h, 4 * ZC)], prs.at[rows(h, 4 * ZC)], sems.at[2 + h])
        c.start()
        copies.append(c)
    for c in copies:
        c.wait()


def table(n):
    k, x = np.arange(n)[:, None], np.arange(n)[None, :]
    return (np.where(k == 0, math.sqrt(1 / n), math.sqrt(2 / n)) * np.cos(math.pi * k * (x + 0.5) / n)).astype(np.float32)


def on_device(modes_now, modes_prev, z_extent, lower_nbr, upper_nbr, x_shift, y_shift):
    slab = modes_now.shape[0]
    flat = jax.ShapeDtypeStruct((slab * ZC, NY), F32)
    cx, cy = table(NX), jnp.asarray(table(NY))
    hbm, vmem = pl.BlockSpec(memory_space=pltpu.HBM), pl.BlockSpec(memory_space=pltpu.VMEM)
    v = lambda *s: pltpu.VMEM(s, F32)
    sm = lambda *s: pltpu.SMEM(s, jnp.int32)
    dma = pltpu.SemaphoreType.DMA
    nxt, cur, y, ztt = pl.pallas_call(
        kernel,
        out_shape=(flat, flat, jax.ShapeDtypeStruct((ZC, 8, NY), F32), jax.ShapeDtypeStruct((ZC, ZC), F32)),
        in_specs=[pl.BlockSpec(memory_space=pltpu.SMEM)] * 3 + [hbm] * 7,
        out_specs=(vmem,) * 4,
        scratch_shapes=[
            sm(1, 2), sm(1, 2), v(512, NY), v(512, NY), v(NX, NX), v(NX, NX), v(NY, NY),
            v(ZC, 8), v(8, ZC), v(24, ZC), v(ZC, 8, NY), v(512, NY), v(512, NY), v(512, NY), v(512, NY), v(512, NY),
            v(64, NY), v(192, NY), v(21, 8, NY), v(6, 8, NY),
            v(2, 6, 8, NY), v(4, 2, 8, NY), v(2, 2, 16, 3, 8, NY), v(2, 2, 4, 3, 8, NY), v(2, 2, 4, 3, 8, NY),
            v(2, 2, 8, 3, 8, NY), v(2, 8, 6, 8, NY), v(2, NX, NX), v(2, NX, NX), v(2, 2, NY, NY), v(6, 8, NY),
            v(2, 8 * NX, NY),
            v(ZC, 8, NY), v(8, 8, 8, NY), v(ZC, NX, NY), v(ZC, NX, NY), v(8, 8, 8, NY), v(ZC, 8, NY),
            dma((7,)), dma, dma, dma((2, 2)), dma((2, 2)), dma((2, 2)), dma((2, 2)),
            dma((2, 2)), dma((2, 2)), dma((2,)), dma((2,)), dma, dma, dma, dma,
        ],
        compiler_params=pltpu.CompilerParams(collective_id=0, has_side_effects=True, vmem_limit_bytes=20 * 2**20),
    )(z_extent, lower_nbr, upper_nbr, *[
        pltpu.with_memory_space_constraint(a, pltpu.HBM)
        for a in (
            x_shift, y_shift,
            modes_now.reshape(slab * ZC, NY), modes_prev.reshape(slab * ZC, NY),
            jnp.asarray(cx), jnp.asarray(cx.T.copy()), cy,
        )
    ])
    anyw = pl.BlockSpec(memory_space=pl.ANY)
    outs = pl.pallas_call(
        finish,
        out_shape=(flat,) * 3,
        in_specs=[anyw, anyw, vmem, vmem, vmem],
        out_specs=(hbm,) * 3,
        scratch_shapes=[v(512, NY), dma((4,))],
        compiler_params=pltpu.CompilerParams(vmem_limit_bytes=8 * 2**20),
    )(nxt, cur, y, ztt, cy)
    return tuple(o.reshape(slab, ZC, NY) for o in outs)


def solution(mesh):
    placed = (
        P("split", "dom", None),
        P("split", "dom", None),
        P("dom"),
        P("dom"),
        P("dom"),
        P("dom", None),
        P("dom", None),
    )
    return jax.shard_map(
        on_device,
        mesh=mesh,
        in_specs=placed,
        out_specs=(P("split", "dom", None),) * 3,
        check_vma=False,
    )
```

```python
import math

import jax
import jax.numpy as jnp
import numpy as np
from jax import lax
from jax.experimental import pallas as pl
from jax.experimental.pallas import tpu as pltpu
from jax.sharding import PartitionSpec as P

F32 = jnp.float32
HIGH = lax.Precision.HIGH
XN, ZN, SN = 4, 16, 8
NX, NY, ZC = 64, 128, 64
QUARTER = 0.25
ST1, ST2, ST3 = 270.0 / 180.0, -27.0 / 180.0, 2.0 / 180.0
GAIN = [2.0 * (-1.0) ** n / math.factorial(2 * n + 2) for n in range(12)]
HALF_PI_2 = (math.pi / 2) ** 2
PAIRS = [(a, b) for a in range(6) for b in range(a, 6)]
MESH = pl.DeviceIdType.MESH


def dot(a, b):
    return jnp.dot(a, b, precision=HIGH, preferred_element_type=F32)


def dot_nt(a, b):
    return lax.dot_general(a, b, (((1,), (1,)), ((), ())), precision=HIGH, preferred_element_type=F32)


def gain_of(u):
    g = jnp.full(u.shape, GAIN[-1], F32)
    for c in GAIN[-2::-1]:
        g = g * u + c
    return g


def cos_table(k, x, length):
    n = k * (2.0 * x + 1.0)
    period = 4.0 * length
    rest = n - period * jnp.floor(n / period + 0.5)
    w = (math.pi / 2) * (rest / length)
    u = w * w
    scale = jnp.where(k == 0, jnp.sqrt(1.0 / length), jnp.sqrt(2.0 / length))
    return scale * (1.0 - 0.5 * u * gain_of(u))


def iota(shape, dim):
    return lax.broadcasted_iota(jnp.int32, shape, dim).astype(F32)


def low_rows(q1, q2, q3):
    return [ST1 * q1 + ST2 * q2 + ST3 * q3, ST2 * q1 + ST3 * q2, ST3 * q1]


def rows(i, n=ZC):
    return pl.ds(pl.multiple_of(i * n, n), n)


WINDOWS = [
    sorted([(i, d) for i in range(XN) for d in ds], key=lambda p: min(p[0], XN - p[0]) + abs(p[1]))
    for ds in (range(-1, 3), range(-2, 2))
]
GREET = [(i, d) for d in (-2, 2, -1, 1, 0) for i in (2, 1, 3, 0) if (i, d) != (0, 0)]


def kernel(
    ext, low, upp, xs_, ys_, m0_, m1_, cx_, cxt_, cy_,
    nxt, cur, out, ztt,
    xs, ys, m0, m1, cx, cxt, cy,
    rt, rtt, w2, rtb, mz, b1, gn, h0, base2, sscr, kscr, kt, sb, st, nb, near, sel, far, aa, bb, xa, xb, yab, gb, g,
    hs, hb, ge, e0, yo, yr,
    in_s, nb_s, nb_r, near_s, near_r, far_s, far_r, aa_s, aa_r, bb_s, bb_r, h_s, h_r, y_s, y_r,
):
    dom, me = lax.axis_index("dom"), lax.axis_index("split")
    px, pz = dom // ZN, lax.rem(dom, ZN)

    loads = [
        pltpu.make_async_copy(a, b, in_s.at[n])
        for n, (a, b) in enumerate([(m0_, m0), (xs_, xs), (ys_, ys), (cx_, cx), (cy_, cy), (m1_, m1), (cxt_, cxt)])
    ]
    for c in loads:
        c.start()

    def at(dx, dz):
        return lax.rem(px + dx + XN, XN) * ZN + lax.rem(pz + dz + ZN, ZN)

    def other(t):
        return lax.rem(me + t, SN)

    barrier = pltpu.get_barrier_semaphore()

    def greet(d, s):
        pl.semaphore_signal(barrier, inc=1, device_id=(d, s), device_id_type=MESH)

    for k in (2, 1, 3):
        greet(at(0, 4 * k), me)
    for i, d in GREET:
        greet(at(i, d), me)
    for t in range(1, SN):
        greet(dom, other(t))

    started = []

    def send(src, dst, ss, rs, d, s):
        pltpu.make_async_remote_copy(
            src_ref=src, dst_ref=dst, send_sem=ss, recv_sem=rs, device_id=(d, s), device_id_type=MESH
        ).start()

    def group(whole, ss, rs):
        return pltpu.make_async_remote_copy(
            src_ref=whole, dst_ref=whole, send_sem=ss, recv_sem=rs, device_id=(dom, me), device_id_type=MESH
        )

    def near_group(step, f):
        return group(near.at[step, f, 1:16], near_s.at[step, f], near_r.at[step, f])

    def far_group(step, f):
        return group(far.at[step, f, 1:4], far_s.at[step, f], far_r.at[step, f])

    def aa_group(step, f):
        return group(aa.at[step, f, 0:7], aa_s.at[step, f], aa_r.at[step, f])

    def bb_group(step):
        return group(bb.at[step, 0:7], bb_s.at[step], bb_r.at[step])

    nb_group, h_group, y_group = group(nb.at[1:4], nb_s, nb_r), group(hb.at[0:7], h_s, h_r), group(yr.at[0:56], y_s, y_r)

    def drained(keep=0):
        while len(started) > keep:
            started.pop(0).wait_send()

    length = ext[0].astype(F32)

    def row_of(r):
        return jnp.where(r < 3, r, r + (length - 6.0))

    def row_table(k, r):
        return jnp.where((k < length) & (r < 6), cos_table(k, row_of(r), jnp.full(k.shape, length)), 0.0)

    rtt[...] = row_table(iota((8, ZC), 1), iota((8, ZC), 0))
    lowf, uppf = low[0].astype(F32), upp[0].astype(F32)
    nb[0, 0] = jnp.full((8, 128), lowf)
    nb[0, 1] = jnp.full((8, 128), uppf)
    loads[0].wait()
    for i in range(8):
        sscr[i * 8 : i * 8 + 8, :] = dot(rtt[...], m0[i * ZC : (i + 1) * ZC, :])
    for r in range(6):
        st[0, r] = sscr[pl.ds(r, 8, stride=8), :]
    pl.semaphore_wait(barrier, len(GREET) + 3 + SN - 1)

    def strip_rows(f):
        return slice(3, 6) if f == 0 else slice(0, 3)

    def send_near(step):
        for f in range(2):
            for n in range(15, 0, -1):
                i, d = WINDOWS[f][n]
                send(st.at[step, strip_rows(f)], near.at[step, f, n], near_s.at[step, f], near_r.at[step, f], at(i, d), me)
            started.append(near_group(step, f))

    for k in (2, 1, 3):
        send(nb.at[0], nb.at[k], nb_s, nb_r, at(0, -4 * k), me)
    started.append(nb_group)
    send_near(0)

    for c in loads[1:5]:
        c.wait()

    for f in range(2):
        for c, n, move, is_x in ((cy, NY, ys[0, f], False), (cx, NX, xs[0, f], True)):
            move = move.astype(F32)
            row, col = iota((n, n), 0), iota((n, n), 1)
            put = (col == row + move).astype(F32)
            tab = c[...]
            seen = ((col + move >= 0) & (col + move < n)).astype(F32)
            moved = dot(tab, put)
            b = dot_nt(tab * seen, tab)
            if is_x:
                has = jnp.where(jnp.full((n, n), uppf if f else lowf) >= 0, QUARTER, 0.0)
                xa[f] = dot_nt(moved, tab) * has
                xb[f] = -b * has
            else:
                yab[f, 0] = dot_nt(tab, moved)
                yab[f, 1] = b

    def own_part(step):
        p = [st[step, r] for r in range(6)]
        for f, part in enumerate((low_rows(p[0], p[1], p[2]), low_rows(p[5], p[4], p[3])[::-1])):
            bb[step, me, 3 * f : 3 * f + 3] = dot(jnp.concatenate(part, axis=0), yab[f, 1]).reshape(3, 8, NY)
        for t in range(1, SN):
            send(bb.at[step, me], bb.at[step, me], bb_s.at[step], bb_r.at[step], dom, other(t))
        started.append(bb_group(step))

    def to_far(step, f):
        acc = [[jnp.zeros((8, NY), F32)] * 3 for _ in range(4)]
        rows_f = strip_rows(f)
        near_group(step, f).wait_recv()
        for n, (i, d) in enumerate(WINDOWS[f]):
            if n == 0:
                block = [st[step, r] for r in range(rows_f.start, rows_f.stop)]
            else:
                block = [near[step, f, n, r] for r in range(3)]
            who = at(-i, -d).astype(F32)
            for k in range(4):
                hit = nb[k, f] == who
                acc[k] = [jnp.where(hit, v, a) for v, a in zip(block, acc[k])]
        for k in (2, 1, 3, 0):
            for r in range(3):
                sel[step, f, k, r] = acc[k][r]
            if k:
                send(sel.at[step, f, k], far.at[step, f, k], far_s.at[step, f], far_r.at[step, f], at(0, 4 * k), me)
        started.append(far_group(step, f))

    def from_far(step, f):
        q = [sel[step, f, 0, r] for r in range(3)]
        far_group(step, f).wait_recv()
        for k in (1, 3, 2):
            q = [a + far[step, f, k, r] for r, a in enumerate(q)]
        part = low_rows(*q)[::-1] if f else low_rows(*q[::-1])
        aa[step, f, me] = dot(jnp.concatenate(part, axis=0), yab[f, 0]).reshape(3, 8, NY)
        for t in (4, 3, 5, 2, 6, 1, 7):
            send(aa.at[step, f, me], aa.at[step, f, me], aa_s.at[step, f], aa_r.at[step, f], dom, other(t))
        started.append(aa_group(step, f))

    def theirs(step, r):
        return aa[step, r // 3, :, r % 3].reshape(NX, NY)

    def ours(step, r):
        return bb[step, :, r].reshape(NX, NY)

    def forced(step, i):
        return gn[rows(i), :] * dot(rt[...], g[step, pl.ds(me * 8 + i, 8, stride=NX), :])

    own_part(0)

    kz = iota((ZC, NY), 0)
    live = kz < length
    lv = jnp.full((ZC, NY), length)
    flat = kz / lv
    flat = flat * flat + (iota((ZC, NY), 1) / NY) ** 2

    def twice(i):
        kx = (me * 8 + i).astype(F32) / NX
        return HALF_PI_2 * (flat + kx * kx)

    loads[5].wait()

    def bases(i, _):
        u = twice(i)
        gain = gain_of(u)
        tw = 2.0 - u * gain
        m = jnp.where(live, m0[rows(i), :], 0.0)
        base = tw * m - jnp.where(live, m1[rows(i), :], 0.0)
        mz[rows(i), :] = m
        gn[rows(i), :] = gain
        b1[rows(i), :] = base
        h0[rows(i), :] = tw * base - m
        return 0

    lax.fori_loop(0, 8, bases, 0)
    nb_group.wait_recv()
    to_far(0, 0)
    to_far(0, 1)

    def turn(k, _):
        hs[k] = h0[pl.ds(k, 8, stride=ZC), :]
        return 0

    lax.fori_loop(0, ZC, turn, 0, unroll=8)

    for t in range(1, SN):
        send(hs.at[rows(other(t), 8)], hb.at[me], h_s, h_r, dom, other(t))
    started.append(h_group)
    hb[me] = hs[rows(me, 8)]
    for n, (a, b) in enumerate(PAIRS):
        w2[n : n + 1, :] = rtt[a : a + 1, :] * rtt[b : b + 1, :]
    w2[21:24, :] = jnp.zeros((3, ZC), F32)

    def strips(i, _):
        sscr[rows(i, 8), :] = dot(rtt[...], b1[rows(i), :])
        kscr[rows(i, 24), :] = dot(w2[...], gn[rows(i), :])
        return 0

    lax.fori_loop(0, 8, strips, 0)
    for r in range(6):
        sb[r] = sscr[pl.ds(r, 8, stride=8), :]
    for n in range(21):
        kt[n] = kscr[pl.ds(n, 8, stride=24), :]
    kx2 = (iota((NX, NY), 0) / NX) ** 2 + (iota((NX, NY), 1) / NY) ** 2

    def angles(k):
        z = jnp.full((NX, NY), k.astype(F32)) / lv
        return HALF_PI_2 * (kx2 + z * z)

    def gains(k, _):
        ge[k] = gain_of(angles(k))
        return 0

    lax.fori_loop(0, ZC, gains, 0)
    bb_group(0).wait_recv()
    for r in range(6):
        gb[r] = dot(xb[r // 3, rows(me, 8), :], ours(0, r))
    from_far(0, 0)
    from_far(0, 1)

    rt[...] = row_table(iota((ZC, 8), 0), iota((ZC, 8), 1))
    kk, zz = iota((ZC, ZC), 1), iota((ZC, ZC), 0)
    ztt[...] = jnp.where((kk < length) & (zz < length), cos_table(kk, zz, jnp.full((ZC, ZC), length)), 0.0)
    g1 = []
    for f in range(2):
        aa_group(0, f).wait_recv()
        for r in range(3 * f, 3 * f + 3):
            g1.append(gb[r] + dot(xa[f, rows(me, 8), :], theirs(0, r)))
    for r in range(6):
        s = sb[r]
        for q in range(6):
            s = s + kt[PAIRS.index((min(r, q), max(r, q)))] * g1[q]
        st[1, r] = s
    send_near(1)
    own_part(1)
    for step in range(2):
        g[step, 6 * NX :, :] = jnp.zeros((2 * NX, NY), F32)
    for r in range(6):
        g[0, r * NX : (r + 1) * NX, :] = dot(xb[r // 3], ours(0, r)) + dot(xa[r // 3], theirs(0, r))
    shape = (ZC, 8, NY)
    rtb[...] = row_table(iota(shape, 0), iota(shape, 1))
    h_group.wait_recv()
    loads[6].wait()

    def early(j, _):
        k = me * 8 + j
        gain = ge[k]
        total = rtb[k, 0:1, :] * g[0, 0:NX, :]
        for r in range(1, 6):
            total = total + rtb[k, r : r + 1, :] * g[0, r * NX : (r + 1) * NX, :]
        e = hb[:, j].reshape(NX, NY) + gain * (2.0 - angles(k) * gain) * total
        yo[:, j] = dot(cxt[...], e).reshape(SN, 8, NY)
        return 0

    lax.fori_loop(0, 8, early, 0)
    to_far(1, 0)
    to_far(1, 1)

    def step_one(i, _):
        m = b1[rows(i), :] + forced(0, i)
        cur[rows(i), :] = m
        base2[rows(i), :] = (2.0 - twice(i) * gn[rows(i), :]) * m - mz[rows(i), :]
        return 0

    drained()
    for t in range(1, SN):
        send(yo.at[other(t)], yr.at[rows(me, 8)], y_s, y_r, dom, other(t))
    started.append(y_group)
    yr[rows(me, 8)] = yo[me]
    bb_group(1).wait_recv()
    for r in range(6):
        g[1, r * NX : (r + 1) * NX, :] = dot(xb[r // 3], ours(1, r))
    lax.fori_loop(0, 8, step_one, 0)
    y_group.wait_recv()
    from_far(1, 0)
    from_far(1, 1)
    drained(2)

    def face(f):
        aa_group(1, f).wait_recv()
        for r in range(3 * f, 3 * f + 3):
            g[1, r * NX : (r + 1) * NX, :] += dot(xa[f], theirs(1, r))

    def weights(k, f):
        return [jnp.broadcast_to(rtb[k, 3 * f + r : 3 * f + r + 1, :], (8, NY)) for r in range(3)]

    def sources(f, x):
        return [g[1, r * NX + x * 8 : r * NX + x * 8 + 8, :] for r in range(3 * f, 3 * f + 3)]

    face(0)

    def lower_part(i, _):
        ws = [weights(i * 4 + n, 0) for n in range(4)]
        for x in range(8):
            src = sources(0, x)
            for n, w in enumerate(ws):
                e0[i * 4 + n, x * 8 : x * 8 + 8, :] = w[0] * src[0] + w[1] * src[1] + w[2] * src[2]
        return 0

    lax.fori_loop(0, ZC // 4, lower_part, 0)
    face(1)
    cx8 = cxt[rows(me, 8), :]
    for i in range(8):
        nxt[i * ZC : (i + 1) * ZC, :] = base2[i * ZC : (i + 1) * ZC, :] + forced(1, i)

    def late(i, _):
        parts = []
        for j in range(0, 8, 4):
            ws = [weights(i * 8 + j + n, 1) for n in range(4)]
            tiles = [[] for _ in ws]
            for x in range(8):
                src = sources(1, x)
                at_x = slice(x * 8, x * 8 + 8)
                for n, w in enumerate(ws):
                    k = i * 8 + j + n
                    total = e0[k, at_x, :] + w[0] * src[0] + w[1] * src[1] + w[2] * src[2]
                    tiles[n].append(ge[k, at_x, :] * total)
            parts += [jnp.concatenate(t, axis=0) for t in tiles]
        x = dot(cx8, jnp.concatenate(parts, axis=1))
        for j in range(8):
            out[i * 8 + j] = yr[i * 8 + j] + x[:, j * NY : (j + 1) * NY]
        return 0

    for i in range(8):
        late(i, 0)
    drained()


def finish(nxt_, cur_, y, ztt, cy, nxt, cur, prs, p, sems):
    copies = [pltpu.make_async_copy(nxt_, nxt, sems.at[0]), pltpu.make_async_copy(cur_, cur, sems.at[1])]
    for c in copies:
        c.start()
    for h in range(4):
        a = dot(ztt[...], jnp.concatenate([y[:, i, :] for i in range(h * 2, h * 2 + 2)], axis=1))
        a = jnp.concatenate([a[:, n * NY : (n + 1) * NY] for n in range(2)], axis=0)
        p[h * 2 * ZC : (h + 1) * 2 * ZC, :] = dot(a, cy[...])
        c = pltpu.make_async_copy(p.at[rows(h, 2 * ZC)], prs.at[rows(h, 2 * ZC)], sems.at[2 + h])
        c.start()
        copies.append(c)
    for c in copies:
        c.wait()


def table(n):
    k, x = np.arange(n)[:, None], np.arange(n)[None, :]
    return (np.where(k == 0, math.sqrt(1 / n), math.sqrt(2 / n)) * np.cos(math.pi * k * (x + 0.5) / n)).astype(np.float32)


def on_device(modes_now, modes_prev, z_extent, lower_nbr, upper_nbr, x_shift, y_shift):
    slab = modes_now.shape[0]
    flat = jax.ShapeDtypeStruct((slab * ZC, NY), F32)
    cx, cy = table(NX), jnp.asarray(table(NY))
    hbm, vmem = pl.BlockSpec(memory_space=pltpu.HBM), pl.BlockSpec(memory_space=pltpu.VMEM)
    v = lambda *s: pltpu.VMEM(s, F32)
    sm = lambda *s: pltpu.SMEM(s, jnp.int32)
    dma = pltpu.SemaphoreType.DMA
    nxt, cur, y, ztt = pl.pallas_call(
        kernel,
        out_shape=(flat, flat, jax.ShapeDtypeStruct((ZC, 8, NY), F32), jax.ShapeDtypeStruct((ZC, ZC), F32)),
        in_specs=[pl.BlockSpec(memory_space=pltpu.SMEM)] * 3 + [hbm] * 7,
        out_specs=(vmem,) * 4,
        scratch_shapes=[
            sm(1, 2), sm(1, 2), v(512, NY), v(512, NY), v(NX, NX), v(NX, NX), v(NY, NY),
            v(ZC, 8), v(8, ZC), v(24, ZC), v(ZC, 8, NY), v(512, NY), v(512, NY), v(512, NY), v(512, NY), v(512, NY),
            v(64, NY), v(192, NY), v(21, 8, NY), v(6, 8, NY),
            v(2, 6, 8, NY), v(4, 2, 8, NY), v(2, 2, 16, 3, 8, NY), v(2, 2, 4, 3, 8, NY), v(2, 2, 4, 3, 8, NY),
            v(2, 2, 8, 3, 8, NY), v(2, 8, 6, 8, NY), v(2, NX, NX), v(2, NX, NX), v(2, 2, NY, NY), v(6, 8, NY),
            v(2, 8 * NX, NY),
            v(ZC, 8, NY), v(8, 8, 8, NY), v(ZC, NX, NY), v(ZC, NX, NY), v(8, 8, 8, NY), v(ZC, 8, NY),
            dma((7,)), dma, dma, dma((2, 2)), dma((2, 2)), dma((2, 2)), dma((2, 2)),
            dma((2, 2)), dma((2, 2)), dma((2,)), dma((2,)), dma, dma, dma, dma,
        ],
        compiler_params=pltpu.CompilerParams(collective_id=0, has_side_effects=True, vmem_limit_bytes=20 * 2**20),
    )(z_extent, lower_nbr, upper_nbr, *[
        pltpu.with_memory_space_constraint(a, pltpu.HBM)
        for a in (
            x_shift, y_shift,
            modes_now.reshape(slab * ZC, NY), modes_prev.reshape(slab * ZC, NY),
            jnp.asarray(cx), jnp.asarray(cx.T.copy()), cy,
        )
    ])
    anyw = pl.BlockSpec(memory_space=pl.ANY)
    outs = pl.pallas_call(
        finish,
        out_shape=(flat,) * 3,
        in_specs=[anyw, anyw, vmem, vmem, vmem],
        out_specs=(hbm,) * 3,
        scratch_shapes=[v(512, NY), dma((6,))],
        compiler_params=pltpu.CompilerParams(vmem_limit_bytes=8 * 2**20),
    )(nxt, cur, y, ztt, cy)
    return tuple(o.reshape(slab, ZC, NY) for o in outs)


def solution(mesh):
    placed = (
        P("split", "dom", None),
        P("split", "dom", None),
        P("dom"),
        P("dom"),
        P("dom"),
        P("dom", None),
        P("dom", None),
    )
    return jax.shard_map(
        on_device,
        mesh=mesh,
        in_specs=placed,
        out_specs=(P("split", "dom", None),) * 3,
        check_vma=False,
    )
```

```python
import math

import jax
import jax.numpy as jnp
import numpy as np
from jax import lax
from jax.experimental import pallas as pl
from jax.experimental.pallas import tpu as pltpu
from jax.sharding import PartitionSpec as P

F32 = jnp.float32
HIGH = lax.Precision.HIGH
XN, ZN, SN = 4, 16, 8
NX, NY, ZC = 64, 128, 64
QUARTER = 0.25
ST1, ST2, ST3 = 270.0 / 180.0, -27.0 / 180.0, 2.0 / 180.0
GAIN = [2.0 * (-1.0) ** n / math.factorial(2 * n + 2) for n in range(12)]
HALF_PI_2 = (math.pi / 2) ** 2
PAIRS = [(a, b) for a in range(6) for b in range(a, 6)]
MESH = pl.DeviceIdType.MESH


def dot(a, b):
    return jnp.dot(a, b, precision=HIGH, preferred_element_type=F32)


def dot_nt(a, b):
    return lax.dot_general(a, b, (((1,), (1,)), ((), ())), precision=HIGH, preferred_element_type=F32)


def gain_of(u):
    g = jnp.full(u.shape, GAIN[-1], F32)
    for c in GAIN[-2::-1]:
        g = g * u + c
    return g


def cos_table(k, x, length):
    n = k * (2.0 * x + 1.0)
    period = 4.0 * length
    rest = n - period * jnp.floor(n / period + 0.5)
    w = (math.pi / 2) * (rest / length)
    u = w * w
    scale = jnp.where(k == 0, jnp.sqrt(1.0 / length), jnp.sqrt(2.0 / length))
    return scale * (1.0 - 0.5 * u * gain_of(u))


def iota(shape, dim):
    return lax.broadcasted_iota(jnp.int32, shape, dim).astype(F32)


def low_rows(q1, q2, q3):
    return [ST1 * q1 + ST2 * q2 + ST3 * q3, ST2 * q1 + ST3 * q2, ST3 * q1]


def rows(i, n=ZC):
    return pl.ds(pl.multiple_of(i * n, n), n)


WINDOWS = [
    sorted([(i, d) for i in range(XN) for d in ds], key=lambda p: min(p[0], XN - p[0]) + abs(p[1]))
    for ds in (range(-1, 3), range(-2, 2))
]
GREET = [(i, d) for d in (-2, 2, -1, 1, 0) for i in (2, 1, 3, 0) if (i, d) != (0, 0)]


def kernel(
    ext, low, upp, xs_, ys_, m0_, m1_, cx_, cxt_, cy_,
    nxt, cur, out, ztt,
    xs, ys, m0, m1, cx, cxt, cy,
    rt, rtt, w2, rtb, mz, b1, gn, h0, base2, sscr, kscr, kt, sb, st, nb, near, sel, far, aa, bb, xa, xb, yab, gb, g,
    hs, hb, ge, e0, yo, yr,
    in_s, nb_s, nb_r, near_s, near_r, far_s, far_r, aa_s, aa_r, bb_s, bb_r, h_s, h_r, y_s, y_r,
):
    dom, me = lax.axis_index("dom"), lax.axis_index("split")
    px, pz = dom // ZN, lax.rem(dom, ZN)

    loads = [
        pltpu.make_async_copy(a, b, in_s.at[n])
        for n, (a, b) in enumerate([(m0_, m0), (xs_, xs), (ys_, ys), (cx_, cx), (cy_, cy), (m1_, m1), (cxt_, cxt)])
    ]
    for c in loads:
        c.start()

    def at(dx, dz):
        return lax.rem(px + dx + XN, XN) * ZN + lax.rem(pz + dz + ZN, ZN)

    def other(t):
        return lax.rem(me + t, SN)

    barrier = pltpu.get_barrier_semaphore()

    def greet(d, s):
        pl.semaphore_signal(barrier, inc=1, device_id=(d, s), device_id_type=MESH)

    for k in (2, 1, 3):
        greet(at(0, 4 * k), me)
    for i, d in GREET:
        greet(at(i, d), me)
    for t in range(1, SN):
        greet(dom, other(t))

    started = []

    def send(src, dst, ss, rs, d, s):
        pltpu.make_async_remote_copy(
            src_ref=src, dst_ref=dst, send_sem=ss, recv_sem=rs, device_id=(d, s), device_id_type=MESH
        ).start()

    def group(whole, ss, rs):
        return pltpu.make_async_remote_copy(
            src_ref=whole, dst_ref=whole, send_sem=ss, recv_sem=rs, device_id=(dom, me), device_id_type=MESH
        )

    def near_group(step, f):
        return group(near.at[step, f, 1:16], near_s.at[step, f], near_r.at[step, f])

    def far_group(step, f):
        return group(far.at[step, f, 1:4], far_s.at[step, f], far_r.at[step, f])

    def aa_group(step, f):
        return group(aa.at[step, f, 0:7], aa_s.at[step, f], aa_r.at[step, f])

    def bb_group(step):
        return group(bb.at[step, 0:7], bb_s.at[step], bb_r.at[step])

    nb_group, h_group, y_group = group(nb.at[1:4], nb_s, nb_r), group(hb.at[0:7], h_s, h_r), group(yr.at[0:56], y_s, y_r)

    def drained():
        while started:
            started.pop(0).wait_send()

    length = ext[0].astype(F32)

    def row_of(r):
        return jnp.where(r < 3, r, r + (length - 6.0))

    def row_table(k, r):
        return jnp.where((k < length) & (r < 6), cos_table(k, row_of(r), jnp.full(k.shape, length)), 0.0)

    rtt[...] = row_table(iota((8, ZC), 1), iota((8, ZC), 0))
    lowf, uppf = low[0].astype(F32), upp[0].astype(F32)
    nb[0, 0] = jnp.full((8, 128), lowf)
    nb[0, 1] = jnp.full((8, 128), uppf)
    loads[0].wait()
    for i in range(8):
        sscr[i * 8 : i * 8 + 8, :] = dot(rtt[...], m0[i * ZC : (i + 1) * ZC, :])
    for r in range(6):
        st[0, r] = sscr[pl.ds(r, 8, stride=8), :]
    pl.semaphore_wait(barrier, len(GREET) + 3 + SN - 1)

    def strip_rows(f):
        return slice(3, 6) if f == 0 else slice(0, 3)

    def send_near(step):
        for f in range(2):
            for n in range(15, 0, -1):
                i, d = WINDOWS[f][n]
                send(st.at[step, strip_rows(f)], near.at[step, f, n], near_s.at[step, f], near_r.at[step, f], at(i, d), me)
            started.append(near_group(step, f))

    for k in (2, 1, 3):
        send(nb.at[0], nb.at[k], nb_s, nb_r, at(0, -4 * k), me)
    started.append(nb_group)
    send_near(0)

    for c in loads[1:5]:
        c.wait()

    for f in range(2):
        for c, n, move, is_x in ((cy, NY, ys[0, f], False), (cx, NX, xs[0, f], True)):
            move = move.astype(F32)
            row, col = iota((n, n), 0), iota((n, n), 1)
            put = (col == row + move).astype(F32)
            tab = c[...]
            seen = ((col + move >= 0) & (col + move < n)).astype(F32)
            moved = dot(tab, put)
            b = dot_nt(tab * seen, tab)
            if is_x:
                has = jnp.where(jnp.full((n, n), uppf if f else lowf) >= 0, QUARTER, 0.0)
                xa[f] = dot_nt(moved, tab) * has
                xb[f] = -b * has
            else:
                yab[f, 0] = dot_nt(tab, moved)
                yab[f, 1] = b

    def own_part(step):
        p = [st[step, r] for r in range(6)]
        for f, part in enumerate((low_rows(p[0], p[1], p[2]), low_rows(p[5], p[4], p[3])[::-1])):
            bb[step, me, 3 * f : 3 * f + 3] = dot(jnp.concatenate(part, axis=0), yab[f, 1]).reshape(3, 8, NY)
        for t in (4, 3, 5, 2, 6, 1, 7):
            send(bb.at[step, me], bb.at[step, me], bb_s.at[step], bb_r.at[step], dom, other(t))
        started.append(bb_group(step))

    def to_far(step, f):
        acc = [[jnp.zeros((8, NY), F32)] * 3 for _ in range(4)]
        rows_f = strip_rows(f)
        near_group(step, f).wait_recv()
        for n, (i, d) in enumerate(WINDOWS[f]):
            if n == 0:
                block = [st[step, r] for r in range(rows_f.start, rows_f.stop)]
            else:
                block = [near[step, f, n, r] for r in range(3)]
            who = at(-i, -d).astype(F32)
            for k in range(4):
                hit = nb[k, f] == who
                acc[k] = [jnp.where(hit, v, a) for v, a in zip(block, acc[k])]
        for k in (2, 1, 3, 0):
            for r in range(3):
                sel[step, f, k, r] = acc[k][r]
            if k:
                send(sel.at[step, f, k], far.at[step, f, k], far_s.at[step, f], far_r.at[step, f], at(0, 4 * k), me)
        started.append(far_group(step, f))

    def from_far(step, f):
        q = [sel[step, f, 0, r] for r in range(3)]
        far_group(step, f).wait_recv()
        for k in (1, 3, 2):
            q = [a + far[step, f, k, r] for r, a in enumerate(q)]
        part = low_rows(*q)[::-1] if f else low_rows(*q[::-1])
        aa[step, f, me] = dot(jnp.concatenate(part, axis=0), yab[f, 0]).reshape(3, 8, NY)
        for t in (4, 3, 5, 2, 6, 1, 7):
            send(aa.at[step, f, me], aa.at[step, f, me], aa_s.at[step, f], aa_r.at[step, f], dom, other(t))
        started.append(aa_group(step, f))

    def theirs(step, r):
        return aa[step, r // 3, :, r % 3].reshape(NX, NY)

    def ours(step, r):
        return bb[step, :, r].reshape(NX, NY)

    def forced(step, i):
        return gn[rows(i), :] * dot(rt[...], g[step, pl.ds(me * 8 + i, 8, stride=NX), :])

    own_part(0)

    kz = iota((ZC, NY), 0)
    live = kz < length
    lv = jnp.full((ZC, NY), length)
    flat = kz / lv
    flat = flat * flat + (iota((ZC, NY), 1) / NY) ** 2

    def twice(i):
        kx = (me * 8 + i).astype(F32) / NX
        return HALF_PI_2 * (flat + kx * kx)

    loads[5].wait()

    def bases(i, _):
        u = twice(i)
        gain = gain_of(u)
        tw = 2.0 - u * gain
        m = jnp.where(live, m0[rows(i), :], 0.0)
        base = tw * m - jnp.where(live, m1[rows(i), :], 0.0)
        mz[rows(i), :] = m
        gn[rows(i), :] = gain
        b1[rows(i), :] = base
        h0[rows(i), :] = tw * base - m
        return 0

    lax.fori_loop(0, 8, bases, 0)
    nb_group.wait_recv()
    to_far(0, 0)
    to_far(0, 1)

    def turn(k, _):
        hs[k] = h0[pl.ds(k, 8, stride=ZC), :]
        return 0

    lax.fori_loop(0, ZC, turn, 0, unroll=8)

    for t in (4, 3, 5, 2, 6, 1, 7):
        send(hs.at[rows(other(t), 8)], hb.at[me], h_s, h_r, dom, other(t))
    started.append(h_group)
    hb[me] = hs[rows(me, 8)]
    for n, (a, b) in enumerate(PAIRS):
        w2[n : n + 1, :] = rtt[a : a + 1, :] * rtt[b : b + 1, :]
    w2[21:24, :] = jnp.zeros((3, ZC), F32)

    def strips(i, _):
        sscr[rows(i, 8), :] = dot(rtt[...], b1[rows(i), :])
        kscr[rows(i, 24), :] = dot(w2[...], gn[rows(i), :])
        return 0

    lax.fori_loop(0, 8, strips, 0)
    for r in range(6):
        sb[r] = sscr[pl.ds(r, 8, stride=8), :]
    for n in range(21):
        kt[n] = kscr[pl.ds(n, 8, stride=24), :]
    kx2 = (iota((NX, NY), 0) / NX) ** 2 + (iota((NX, NY), 1) / NY) ** 2

    def angles(k):
        z = jnp.full((NX, NY), k.astype(F32)) / lv
        return HALF_PI_2 * (kx2 + z * z)

    def gains(k, _):
        ge[k] = gain_of(angles(k))
        return 0

    lax.fori_loop(0, ZC, gains, 0)
    bb_group(0).wait_recv()
    for r in range(6):
        gb[r] = dot(xb[r // 3, rows(me, 8), :], ours(0, r))
    from_far(0, 0)
    from_far(0, 1)

    rt[...] = row_table(iota((ZC, 8), 0), iota((ZC, 8), 1))
    kk, zz = iota((ZC, ZC), 1), iota((ZC, ZC), 0)
    ztt[...] = jnp.where((kk < length) & (zz < length), cos_table(kk, zz, jnp.full((ZC, ZC), length)), 0.0)
    g1 = []
    for f in range(2):
        aa_group(0, f).wait_recv()
        for r in range(3 * f, 3 * f + 3):
            g1.append(gb[r] + dot(xa[f, rows(me, 8), :], theirs(0, r)))
    for r in range(6):
        s = sb[r]
        for q in range(6):
            s = s + kt[PAIRS.index((min(r, q), max(r, q)))] * g1[q]
        st[1, r] = s
    send_near(1)
    own_part(1)
    for step in range(2):
        g[step, 6 * NX :, :] = jnp.zeros((2 * NX, NY), F32)
    for r in range(6):
        g[0, r * NX : (r + 1) * NX, :] = dot(xb[r // 3], ours(0, r)) + dot(xa[r // 3], theirs(0, r))
    shape = (ZC, 8, NY)
    rtb[...] = row_table(iota(shape, 0), iota(shape, 1))
    h_group.wait_recv()
    loads[6].wait()

    def early(j, _):
        k = me * 8 + j
        gain = ge[k]
        total = rtb[k, 0:1, :] * g[0, 0:NX, :]
        for r in range(1, 6):
            total = total + rtb[k, r : r + 1, :] * g[0, r * NX : (r + 1) * NX, :]
        e = hb[:, j].reshape(NX, NY) + gain * (2.0 - angles(k) * gain) * total
        yo[:, j] = dot(cxt[...], e).reshape(SN, 8, NY)
        return 0

    lax.fori_loop(0, 8, early, 0)
    to_far(1, 0)
    to_far(1, 1)

    def step_one(i, _):
        m = b1[rows(i), :] + forced(0, i)
        cur[rows(i), :] = m
        base2[rows(i), :] = (2.0 - twice(i) * gn[rows(i), :]) * m - mz[rows(i), :]
        return 0

    drained()
    for t in (4, 3, 5, 2, 6, 1, 7):
        send(yo.at[other(t)], yr.at[rows(me, 8)], y_s, y_r, dom, other(t))
    started.append(y_group)
    yr[rows(me, 8)] = yo[me]
    bb_group(1).wait_recv()
    for r in range(6):
        g[1, r * NX : (r + 1) * NX, :] = dot(xb[r // 3], ours(1, r))
    lax.fori_loop(0, 8, step_one, 0)
    y_group.wait_recv()
    from_far(1, 0)
    from_far(1, 1)

    def face(f):
        aa_group(1, f).wait_recv()
        for r in range(3 * f, 3 * f + 3):
            g[1, r * NX : (r + 1) * NX, :] += dot(xa[f], theirs(1, r))

    def weights(k, f):
        return [jnp.broadcast_to(rtb[k, 3 * f + r : 3 * f + r + 1, :], (8, NY)) for r in range(3)]

    def sources(f, x):
        return [g[1, r * NX + x * 8 : r * NX + x * 8 + 8, :] for r in range(3 * f, 3 * f + 3)]

    face(0)

    def lower_part(i, _):
        ws = [weights(i * 4 + n, 0) for n in range(4)]
        for x in range(8):
            src = sources(0, x)
            for n, w in enumerate(ws):
                e0[i * 4 + n, x * 8 : x * 8 + 8, :] = w[0] * src[0] + w[1] * src[1] + w[2] * src[2]
        return 0

    lax.fori_loop(0, ZC // 4, lower_part, 0)
    face(1)
    cx8 = cxt[rows(me, 8), :]
    for i in range(8):
        nxt[i * ZC : (i + 1) * ZC, :] = base2[i * ZC : (i + 1) * ZC, :] + forced(1, i)

    def late(i, _):
        parts = []
        for j in range(0, 8, 4):
            ws = [weights(i * 8 + j + n, 1) for n in range(4)]
            tiles = [[] for _ in ws]
            for x in range(8):
                src = sources(1, x)
                at_x = slice(x * 8, x * 8 + 8)
                for n, w in enumerate(ws):
                    k = i * 8 + j + n
                    total = e0[k, at_x, :] + w[0] * src[0] + w[1] * src[1] + w[2] * src[2]
                    tiles[n].append(ge[k, at_x, :] * total)
            parts += [jnp.concatenate(t, axis=0) for t in tiles]
        x = dot(cx8, jnp.concatenate(parts, axis=1))
        for j in range(8):
            out[i * 8 + j] = yr[i * 8 + j] + x[:, j * NY : (j + 1) * NY]
        return 0

    for i in range(8):
        late(i, 0)
    drained()


def finish(nxt_, cur_, y, ztt, cy, nxt, cur, prs, p, sems):
    copies = [pltpu.make_async_copy(nxt_, nxt, sems.at[0]), pltpu.make_async_copy(cur_, cur, sems.at[1])]
    for c in copies:
        c.start()
    for h in range(4):
        a = dot(ztt[...], jnp.concatenate([y[:, i, :] for i in range(h * 2, h * 2 + 2)], axis=1))
        a = jnp.concatenate([a[:, n * NY : (n + 1) * NY] for n in range(2)], axis=0)
        p[h * 2 * ZC : (h + 1) * 2 * ZC, :] = dot(a, cy[...])
        c = pltpu.make_async_copy(p.at[rows(h, 2 * ZC)], prs.at[rows(h, 2 * ZC)], sems.at[2 + h])
        c.start()
        copies.append(c)
    for c in copies:
        c.wait()


def table(n):
    k, x = np.arange(n)[:, None], np.arange(n)[None, :]
    return (np.where(k == 0, math.sqrt(1 / n), math.sqrt(2 / n)) * np.cos(math.pi * k * (x + 0.5) / n)).astype(np.float32)


def on_device(modes_now, modes_prev, z_extent, lower_nbr, upper_nbr, x_shift, y_shift):
    slab = modes_now.shape[0]
    flat = jax.ShapeDtypeStruct((slab * ZC, NY), F32)
    cx, cy = table(NX), jnp.asarray(table(NY))
    hbm, vmem = pl.BlockSpec(memory_space=pltpu.HBM), pl.BlockSpec(memory_space=pltpu.VMEM)
    v = lambda *s: pltpu.VMEM(s, F32)
    sm = lambda *s: pltpu.SMEM(s, jnp.int32)
    dma = pltpu.SemaphoreType.DMA
    nxt, cur, y, ztt = pl.pallas_call(
        kernel,
        out_shape=(flat, flat, jax.ShapeDtypeStruct((ZC, 8, NY), F32), jax.ShapeDtypeStruct((ZC, ZC), F32)),
        in_specs=[pl.BlockSpec(memory_space=pltpu.SMEM)] * 3 + [hbm] * 7,
        out_specs=(vmem,) * 4,
        scratch_shapes=[
            sm(1, 2), sm(1, 2), v(512, NY), v(512, NY), v(NX, NX), v(NX, NX), v(NY, NY),
            v(ZC, 8), v(8, ZC), v(24, ZC), v(ZC, 8, NY), v(512, NY), v(512, NY), v(512, NY), v(512, NY), v(512, NY),
            v(64, NY), v(192, NY), v(21, 8, NY), v(6, 8, NY),
            v(2, 6, 8, NY), v(4, 2, 8, NY), v(2, 2, 16, 3, 8, NY), v(2, 2, 4, 3, 8, NY), v(2, 2, 4, 3, 8, NY),
            v(2, 2, 8, 3, 8, NY), v(2, 8, 6, 8, NY), v(2, NX, NX), v(2, NX, NX), v(2, 2, NY, NY), v(6, 8, NY),
            v(2, 8 * NX, NY),
            v(ZC, 8, NY), v(8, 8, 8, NY), v(ZC, NX, NY), v(ZC, NX, NY), v(8, 8, 8, NY), v(ZC, 8, NY),
            dma((7,)), dma, dma, dma((2, 2)), dma((2, 2)), dma((2, 2)), dma((2, 2)),
            dma((2, 2)), dma((2, 2)), dma((2,)), dma((2,)), dma, dma, dma, dma,
        ],
        compiler_params=pltpu.CompilerParams(collective_id=0, has_side_effects=True, vmem_limit_bytes=20 * 2**20),
    )(z_extent, lower_nbr, upper_nbr, *[
        pltpu.with_memory_space_constraint(a, pltpu.HBM)
        for a in (
            x_shift, y_shift,
            modes_now.reshape(slab * ZC, NY), modes_prev.reshape(slab * ZC, NY),
            jnp.asarray(cx), jnp.asarray(cx.T.copy()), cy,
        )
    ])
    anyw = pl.BlockSpec(memory_space=pl.ANY)
    outs = pl.pallas_call(
        finish,
        out_shape=(flat,) * 3,
        in_specs=[anyw, anyw, vmem, vmem, vmem],
        out_specs=(hbm,) * 3,
        scratch_shapes=[v(512, NY), dma((6,))],
        compiler_params=pltpu.CompilerParams(vmem_limit_bytes=8 * 2**20),
    )(nxt, cur, y, ztt, cy)
    return tuple(o.reshape(slab, ZC, NY) for o in outs)


def solution(mesh):
    placed = (
        P("split", "dom", None),
        P("split", "dom", None),
        P("dom"),
        P("dom"),
        P("dom"),
        P("dom", None),
        P("dom", None),
    )
    return jax.shard_map(
        on_device,
        mesh=mesh,
        in_specs=placed,
        out_specs=(P("split", "dom", None),) * 3,
        check_vma=False,
    )
```
